256 devices in a mesh: sess: 16 (over z, core), tp: 16 (over y, x).
Axes of the slice: x: 4, y: 4, z: 8, core: 2. Of those that a mesh axis runs over, the one named last changes fastest.
Arguments:
- frames: bfloat16 [256, 4096], P('sess', 'tp'), may hold values from -6 to 6
- norm_gain: bfloat16 [4096], replicated, may hold values from 0.5 to 1.5
- w_qkv: bfloat16 [3, 4096, 2048], P(None, None, 'tp'), may hold values from -0.09375 to 0.09375
- w_out: bfloat16 [2048, 4096], P('tp'), may hold values from -0.5 to 0.5
- kv_cache: bfloat16 [2, 512, 375, 2048], P(None, 'sess', None, 'tp'), may hold values from -800 to 800
- frame_session: int32 [256], replicated, may hold values from 0 to 255, as said below
- owner_of: int32 [256], replicated, may hold values from 0 to 15, as said below
- context_len: int32 [256], replicated, may hold values from 1 to 375, as said below
Outputs:
- hidden_rows: bfloat16 [256, 4096], P('sess', 'tp')
The draws below stay inside these ranges and needn't reach their ends.
Inputs may be any that keep to these rules, and one draw needn't show every extreme that they name: `frame_session`: a permutation of the sessions; at most 2 of the frame rows of one index of sess have the same owner, and some rows reach 2. `owner_of`: each owner holds at most 32 sessions, and some owner holds exactly 32. `context_len`: some session has exactly 375.
All inputs are finite; a program needn't handle non-finite values.
Results may differ from the reference program's by a relative error of at most 0.014.
The reference program's roundings to bfloat16 on the way (of `normed`, `projected`, `weights` and `attended`) count: a program that leaves them out, or rounds other values in their place, can miss the bound.
Values may be sent and summed in bfloat16 or wider, within the bound.
No kernel may reach another device: no remote copies, remote signals or barrier semaphores. Data moves between devices by JAX's collectives and lax.ppermute only.
A program may use at most 64 MiB of HBM per device.

```python
import jax
import jax.numpy as jnp
from jax import lax

D = 4096
HEADS = 16
HD = 128
CTX = 375
SESS_DEV = 16
SESSIONS = 256
SLOTS = 32
N_SESS = 16


def session_layout(key):
    base_key = jax.random.fold_in(key, 7)
    key_heavy, key_offset, key_order = jax.random.split(base_key, 3)
    positions = jnp.arange(SESSIONS, dtype=jnp.int32)
    heavy = jax.random.randint(key_heavy, (), 0, N_SESS, dtype=jnp.int32)
    offset = jax.random.randint(key_offset, (), 0, N_SESS, dtype=jnp.int32)
    order = jax.random.permutation(key_order, SESSIONS).astype(jnp.int32)
    others = (positions - SLOTS) % (N_SESS - 1)
    owner_pos = jnp.where(positions < SLOTS, heavy, others + (others >= heavy).astype(jnp.int32))
    row_pos = (positions + offset) % N_SESS * SESS_DEV + positions // N_SESS
    frame_session = jnp.zeros((SESSIONS,), jnp.int32).at[row_pos].set(order)
    owner_of = jnp.zeros((SESSIONS,), jnp.int32).at[order].set(owner_pos.astype(jnp.int32))
    return (frame_session, owner_of)


def draw_frame_session(key, part):
    return session_layout(key)[0]


def draw_owner_of(key, part):
    return session_layout(key)[1]


def draw_context_len(key, part):
    lengths = jax.random.randint(jax.random.fold_in(key, 11), (SESSIONS,), 1, CTX + 1, dtype=jnp.int32)
    longest = jax.random.randint(jax.random.fold_in(key, 12), (), 0, SESSIONS, dtype=jnp.int32)
    return lengths.at[longest].set(CTX)


def draw_kv_cache(key, part):
    key_base = jax.random.fold_in(jax.random.fold_in(key, 13), 0)
    slot_total = N_SESS * SLOTS
    shape = (2, slot_total, CTX, HEADS * HD)
    scale = jnp.array([1.0, 2.0], jnp.float32)[:, None, None, None]
    whole = jnp.clip(jax.random.normal(key_base, shape, jnp.float32), -4.0, 4.0) * scale
    return whole.astype(jnp.bfloat16)


def block_scale(rng, extent, pieces, low, largest):
    def one(axis_at, shards_of):
        heights = jax.random.uniform(jax.random.fold_in(jax.random.fold_in(rng, 6), axis_at), (shards_of,), jnp.float32, low / len(pieces), largest / len(pieces))
        return jnp.repeat(jnp.exp(heights), extent[axis_at] // shards_of).reshape((-1,) + (1,) * (len(extent) - axis_at - 1))

    gain = one(*pieces[0])
    for cut in pieces[1:]:
        gain = gain * one(*cut)
    return gain


def scatter_about(own_key, shape, width, reach, cuts=(), held_as=jnp.bfloat16):
    gain = block_scale(own_key, shape, cuts, -0.22, 0.18) if cuts else 1.0
    values = jax.random.normal(own_key, shape, jnp.float32) * width * gain
    return jnp.minimum(jnp.maximum(values, -reach), reach).astype(held_as)


def setup_inputs(seed: int = 0) -> dict:
    key_of = jax.random.split(jax.random.key(seed), 9)
    return {
        "frames": scatter_about(key_of[0], (SESSIONS, D), 1.0, 6.0, ((0, 16), (1, 16))),
        "norm_gain": jnp.clip(1.0 + 0.1 * jax.random.normal(key_of[1], (D,), jnp.float32), 0.5, 1.5).astype(jnp.bfloat16),
        "w_qkv": scatter_about(key_of[2], (3, D, HEADS * HD), D ** -0.5, 0.09375, ((2, 16),)),
        "w_out": scatter_about(key_of[3], (HEADS * HD, D), HD ** -0.5, 0.5, ((0, 16),)),
        "kv_cache": draw_kv_cache(jax.random.fold_in(key_of[8], 71), 0),
        "frame_session": draw_frame_session(jax.random.fold_in(key_of[8], 71), 0),
        "owner_of": draw_owner_of(jax.random.fold_in(key_of[8], 71), 0),
        "context_len": draw_context_len(jax.random.fold_in(key_of[8], 71), 0),
    }


def attend_row(triple, cached, length):
    heads_count = triple.shape[1] // HD
    queries = triple[0].astype(jnp.float32).reshape(heads_count, HD)
    new_keys = triple[1].astype(jnp.float32).reshape(heads_count, HD)
    new_values = triple[2].astype(jnp.float32).reshape(heads_count, HD)
    cached_keys = cached[0].astype(jnp.float32).reshape(CTX, heads_count, HD)
    cached_values = cached[1].astype(jnp.float32).reshape(CTX, heads_count, HD)
    factor = 1.0 / jnp.sqrt(jnp.float32(HD))
    scores = jnp.einsum('hd,thd->ht', queries, cached_keys) * factor
    own_score = lax.optimization_barrier(jnp.sum(queries * new_keys, axis=-1)) * factor
    valid = jnp.arange(CTX, dtype=jnp.int32)[None, :] < length
    scores = jnp.where(valid, scores, -jnp.inf)
    top_score = jnp.maximum(lax.optimization_barrier(jnp.max(scores, axis=-1)), own_score)
    expo = jnp.where(valid, jnp.exp(scores - top_score[:, None]), 0.0)
    own_exp = jnp.exp(own_score - top_score)
    total = lax.optimization_barrier(jnp.sum(expo, axis=-1)) + own_exp
    weights = (expo / total[:, None]).astype(jnp.bfloat16).astype(jnp.float32)
    own_weight = (own_exp / total).astype(jnp.bfloat16).astype(jnp.float32)
    mixed = jnp.einsum('ht,thd->hd', weights, cached_values) + own_weight[:, None] * new_values
    return mixed.astype(jnp.bfloat16).reshape(heads_count * HD)

def reference(frames, norm_gain, w_qkv, w_out, kv_cache, frame_session, owner_of, context_len):
    wide = frames.astype(jnp.float32)
    normed = (wide * lax.rsqrt(lax.optimization_barrier(jnp.mean(wide * wide, axis=1, keepdims=True)) + 1e-05) * norm_gain.astype(jnp.float32)).astype(jnp.bfloat16)
    projected = jnp.einsum('rd,cde->rce', normed.astype(jnp.float32), w_qkv.astype(jnp.float32)).astype(jnp.bfloat16)
    session_ids = jnp.arange(SESSIONS, dtype=jnp.int32)
    same_owner = owner_of[:, None] == owner_of[None, :]
    slot_of = lax.optimization_barrier(jnp.sum(same_owner & (session_ids[None, :] < session_ids[:, None]), axis=1)).astype(jnp.int32)
    cache_row = (owner_of * SLOTS + slot_of)[frame_session].astype(jnp.int32)
    row_length = context_len[frame_session].astype(jnp.int32)

    def one_row(packed):
        triple, crow, length = packed
        cached = lax.dynamic_index_in_dim(kv_cache, crow, 1, keepdims=False)
        return attend_row(triple, cached, length)
    attended = lax.map(one_row, (projected, cache_row, row_length))
    branch = jnp.dot(attended, w_out, preferred_element_type=jnp.float32)
    return (wide + branch).astype(jnp.bfloat16)
```

```python
import jax
import jax.numpy as jnp
from jax import lax
from jax.experimental import pallas as pl
from jax.experimental.pallas import tpu as pltpu
from jax.sharding import PartitionSpec as P

HD = 128
BF = jnp.bfloat16
F32 = jnp.float32
VM = pl.BlockSpec(memory_space=pltpu.VMEM)
SM = pl.BlockSpec(memory_space=pltpu.SMEM)


def row_targets(session_ref, owner_ref, block, rows, cap, count_ref, owners):
    for o in range(owners):
        count_ref[o] = 0
    targets = []
    for r in range(rows):
        o = owner_ref[session_ref[block * rows + r]]
        pair = count_ref[o]
        count_ref[o] = pair + 1
        targets.append(o * cap + pair)
    return targets


def dispatch_kernel(block_ref, session_ref, owner_ref, frames_ref, out_ref, held, count_ref):
    rows = frames_ref.shape[0]
    owners, peers, cap, width = out_ref.shape
    held[...] = jnp.zeros_like(held)
    wide = frames_ref[...].astype(F32)
    targets = row_targets(session_ref, owner_ref, block_ref[0], rows, cap, count_ref, owners)
    for r in range(rows):
        held[pl.ds(targets[r], 1), :] = wide[r : r + 1]
    for o in range(owners):
        pair = held[o * cap : (o + 1) * cap, :].astype(BF)
        out_ref[o] = jnp.broadcast_to(pair[None], (peers, cap, width))


def attend_kernel(
    x_ref, gain_ref, w_ref, kv_ref, w_out_ref, collect_ref, place_ref, length_ref,
    out_ref, rows_ref, score_ref, spread_ref,
):
    owners, peers, cap, width = x_ref.shape
    places = owners * cap
    model = peers * width
    context, slots = kv_ref.shape[1], kv_ref.shape[2]
    group = HD // slots
    steps = (context + group) // group
    for s in range(owners):
        for t in range(peers):
            rows_ref[s * cap : (s + 1) * cap, t * width : (t + 1) * width] = x_ref[s, t]
    wide = rows_ref[...].astype(F32)
    scale = lax.rsqrt(jnp.sum(wide * wide, axis=1, keepdims=True) / model + 1e-05)
    normed = (wide * scale * gain_ref[...]).astype(BF)
    projected = [
        jnp.dot(normed, w_ref[c], preferred_element_type=F32).astype(BF) for c in range(3)
    ]
    collect = collect_ref[...]
    query, new_key, new_value = [
        jnp.dot(collect, p, preferred_element_type=F32).astype(BF) for p in projected
    ]
    lane = lax.broadcasted_iota(jnp.int32, (slots, HD), 1)
    own = lax.broadcasted_iota(jnp.int32, (slots, HD), 0) == lane % slots
    for g in range(steps):
        if g < steps - 1:
            keys = kv_ref[0, g * group : (g + 1) * group].reshape(HD, HD)
        else:
            tail = kv_ref[0, g * group : context].reshape(HD - slots, HD)
            keys = jnp.concatenate([tail, new_key], axis=0)
        dots = lax.dot_general(
            query, keys, (((1,), (1,)), ((), ())), preferred_element_type=F32
        )
        score_ref[g : g + 1, :] = jnp.sum(jnp.where(own, dots, 0.0), axis=0, keepdims=True)
    scores = score_ref[0:steps, :] * (1.0 / jnp.sqrt(F32(HD)))
    lanes = lax.broadcasted_iota(jnp.int32, (steps, HD), 1)
    frame = lax.broadcasted_iota(jnp.int32, (steps, HD), 0) * group + lanes // slots
    valid = (frame < length_ref[...]) | (frame == context)
    scores = jnp.where(valid, scores, -jnp.inf)
    top = jnp.max(scores, axis=0, keepdims=True)
    shift = slots
    while shift < HD:
        top = jnp.maximum(top, pltpu.roll(top, shift, 1))
        shift *= 2
    expo = jnp.where(valid, jnp.exp(scores - top), 0.0)
    total = jnp.sum(expo, axis=0, keepdims=True)
    shift = slots
    while shift < HD:
        total = total + pltpu.roll(total, shift, 1)
        shift *= 2
    score_ref[0:steps, :] = expo / total
    place = place_ref[...] > 0.0
    mixed = jnp.zeros((places, HD), F32)
    for g in range(steps):
        weights = jnp.where(place, score_ref[g : g + 1, :], 0.0).astype(BF)
        if g < steps - 1:
            values = kv_ref[1, g * group : (g + 1) * group].reshape(HD, HD)
        else:
            tail = kv_ref[1, g * group : context].reshape(HD - slots, HD)
            values = jnp.concatenate([tail, new_value], axis=0)
        mixed += jnp.dot(weights, values, preferred_element_type=F32)
    attended = mixed.astype(BF)
    for t in range(peers):
        part = jnp.dot(
            attended, w_out_ref[:, t * width : (t + 1) * width], preferred_element_type=F32
        ).astype(BF)
        for s in range(owners):
            out_ref[s, t] = part[s * cap : (s + 1) * cap]


def finish_kernel(block_ref, session_ref, owner_ref, parts_ref, frames_ref, out_ref, held, sums, count_ref):
    rows = frames_ref.shape[0]
    owners, peers, cap, width = parts_ref.shape
    targets = row_targets(session_ref, owner_ref, block_ref[0], rows, cap, count_ref, owners)
    for o in range(owners):
        held[o * cap : (o + 1) * cap, :] = jnp.sum(parts_ref[o].astype(F32), axis=0)
    for r in range(rows):
        sums[r : r + 1, :] = held[pl.ds(targets[r], 1), :]
    out_ref[...] = (frames_ref[...].astype(F32) + sums[...]).astype(BF)


def body(frames, norm_gain, w_qkv, w_out, kv_cache, frame_session, owner_of, context_len):
    owners = lax.axis_size("sess")
    peers = lax.axis_size("tp")
    me = lax.axis_index("sess")
    rows, width = frames.shape
    slots = kv_cache.shape[1]
    sessions = frame_session.shape[0]
    cap = (slots + owners - 1) // owners
    places = owners * cap
    block = me.reshape(1).astype(jnp.int32)
    exchange = (owners, peers, cap, width)

    outgoing = pl.pallas_call(
        dispatch_kernel,
        out_shape=jax.ShapeDtypeStruct(exchange, BF),
        in_specs=[SM, SM, SM, VM],
        out_specs=VM,
        scratch_shapes=[pltpu.VMEM((places, width), F32), pltpu.SMEM((owners,), jnp.int32)],
        name="dispatch",
    )(block, frame_session, owner_of, frames)
    arrived = lax.all_to_all(
        outgoing.reshape(owners * peers, cap, width),
        ("sess", "tp"), split_axis=0, concat_axis=0, tiled=True,
    ).reshape(exchange)

    session_ids = jnp.arange(sessions, dtype=jnp.int32)
    mine = owner_of == me
    slot_of = jnp.sum(mine[None, :] & (session_ids[None, :] < session_ids[:, None]), axis=1)
    matches = frame_session[:, None] == session_ids[None, :]
    row_mine = jnp.any(matches & mine[None, :], axis=1)
    row_slot = jnp.sum(jnp.where(matches, slot_of[None, :], 0), axis=1)
    row_block = session_ids // rows
    earlier = (row_block[:, None] == row_block[None, :]) & (session_ids[None, :] < session_ids[:, None])
    row_pair = jnp.sum(earlier & row_mine[None, :], axis=1)
    row_place = jnp.where(row_mine, row_block * cap + row_pair, -1)
    place_ids = jnp.arange(places, dtype=jnp.int32)
    at_place = row_place[None, :] == place_ids[:, None]
    place_slot = jnp.sum(jnp.where(at_place, row_slot[None, :] + 1, 0), axis=1) - 1
    slot_ids = jnp.arange(slots, dtype=jnp.int32)
    collect = (slot_ids[:, None] == place_slot[None, :]).astype(BF)
    lane_slot = jnp.arange(HD, dtype=jnp.int32) % slots
    place_mask = (place_slot[:, None] == lane_slot[None, :]).astype(F32)
    lane_session = mine[:, None] & (slot_of[:, None] == lane_slot[None, :])
    lengths = jnp.sum(jnp.where(lane_session, context_len[:, None], 0), axis=0)[None, :]

    context = kv_cache.shape[2]
    steps = (context + HD // slots) // (HD // slots)
    partial_rows = pl.pallas_call(
        attend_kernel,
        out_shape=jax.ShapeDtypeStruct(exchange, BF),
        in_specs=[VM] * 8,
        out_specs=VM,
        scratch_shapes=[
            pltpu.VMEM((places, peers * width), BF),
            pltpu.VMEM((steps + (-steps) % 8, HD), F32),
            pltpu.VMEM((8, HD), F32),
        ],
        name="attend",
    )(
        arrived,
        norm_gain.astype(F32).reshape(1, -1),
        w_qkv,
        kv_cache.transpose(0, 2, 1, 3),
        w_out,
        collect,
        place_mask,
        lengths,
    )
    parts = lax.all_to_all(
        partial_rows.reshape(owners * peers, cap, width),
        ("sess", "tp"), split_axis=0, concat_axis=0, tiled=True,
    ).reshape(exchange)
    return pl.pallas_call(
        finish_kernel,
        out_shape=jax.ShapeDtypeStruct(frames.shape, frames.dtype),
        in_specs=[SM, SM, SM, VM, VM],
        out_specs=VM,
        scratch_shapes=[
            pltpu.VMEM((places, width), F32),
            pltpu.VMEM((rows, width), F32),
            pltpu.SMEM((owners,), jnp.int32),
        ],
        name="finish",
    )(block, frame_session, owner_of, parts, frames)


def solution(mesh):
    in_specs = (
        P("sess", "tp"),
        P(),
        P(None, None, "tp"),
        P("tp", None),
        P(None, "sess", None, "tp"),
        P(),
        P(),
        P(),
    )
    out_specs = P("sess", "tp")
    return jax.shard_map(body, mesh=mesh, in_specs=in_specs, out_specs=out_specs, check_vma=False)
```

```python
import functools

import jax
import jax.numpy as jnp
from jax import lax
from jax.experimental import pallas as pl
from jax.experimental.pallas import tpu as pltpu
from jax.sharding import PartitionSpec as P

HD = 128
BF = jnp.bfloat16
F32 = jnp.float32
VM = pl.BlockSpec(memory_space=pltpu.VMEM)
SM = pl.BlockSpec(memory_space=pltpu.SMEM)


def near(*arrays):
    return [pltpu.with_memory_space_constraint(a, pltpu.VMEM) for a in arrays]


def row_targets(session_ref, owner_ref, block, rows, cap, count_ref, owners):
    for o in range(owners):
        count_ref[o] = 0
    targets = []
    for r in range(rows):
        o = owner_ref[session_ref[block * rows + r]]
        pair = count_ref[o]
        count_ref[o] = pair + 1
        targets.append(o * cap + pair)
    return targets


def dispatch_kernel(block_ref, session_ref, owner_ref, frames_ref, out_ref, held, count_ref):
    rows = frames_ref.shape[0]
    owners, peers, cap, width = out_ref.shape
    held[...] = jnp.zeros_like(held)
    wide = frames_ref[...].astype(F32)
    targets = row_targets(session_ref, owner_ref, block_ref[0], rows, cap, count_ref, owners)
    for r in range(rows):
        held[pl.ds(targets[r], 1), :] = wide[r : r + 1]
    for o in range(owners):
        pair = held[o * cap : (o + 1) * cap, :].astype(BF)
        out_ref[o] = jnp.broadcast_to(pair[None], (peers, cap, width))


def table_kernel(
    blocks, block_ref, session_ref, owner_ref, length_ref, gain_ref,
    collect_ref, place_ref, lane_length_ref, wide_gain_ref,
):
    wide_gain_ref[...] = gain_ref[...].astype(F32)
    sessions = session_ref.shape[1]
    slots, places = collect_ref.shape
    me = block_ref[0]

    def iota(shape, dim):
        return lax.broadcasted_iota(jnp.int32, shape, dim)

    def dot(a, b, dims):
        return lax.dot_general(
            a.astype(BF), b.astype(BF), (dims, ((), ())), preferred_element_type=F32
        )

    def one(flag):
        return jnp.where(flag, 1.0, 0.0)

    square = (sessions, sessions)
    before, after = iota(square, 0), iota(square, 1)
    mine = jnp.broadcast_to(one(owner_ref[...] == me), (8, sessions))
    slot_of = dot(mine, one(before < after), ((1,), (0,)))
    rows_per_block = sessions // blocks
    cap = places // blocks
    matches = one(before == session_ref[...])
    row_mine = dot(mine, matches, ((1,), (0,)))
    row_slot = dot(slot_of, matches, ((1,), (0,)))[0:1].astype(jnp.int32)
    same_block = (before // rows_per_block == after // rows_per_block) & (before < after)
    row_pair = dot(row_mine, one(same_block), ((1,), (0,)))[0:1].astype(jnp.int32)
    owned = row_mine[0:1] > 0.5
    row_place = iota((1, sessions), 1) // rows_per_block * cap + row_pair
    at_place = (iota((places, sessions), 0) == row_place) & owned
    at_slot = (iota((slots, sessions), 0) == row_slot) & owned
    collect_ref[...] = dot(one(at_slot), one(at_place), ((1,), (1,))).astype(BF)
    place_slot = jnp.sum(jnp.where(at_place, row_slot + 1, 0), axis=1, keepdims=True) - 1
    place_ref[...] = one(place_slot == iota((places, HD), 1) % slots)
    lane_session = one(
        (iota((HD, sessions), 0) % slots == slot_of[0:1].astype(jnp.int32)) & (mine[0:1] > 0.5)
    )
    length = jnp.broadcast_to(length_ref[...], (8, sessions))
    high = dot((length >> 4).astype(F32), lane_session, ((1,), (1,)))
    low = dot((length & 15).astype(F32), lane_session, ((1,), (1,)))
    lane_length_ref[...] = (high * 16.0 + low)[0:1].astype(jnp.int32)


def attend_kernel(
    x_ref, w_ref, collect_ref, place_ref, length_ref, gain_ref, kv_hbm, w_out_hbm,
    out_ref, kv_ref, w_out_ref, sems, rows_ref, score_ref,
):
    copies = [
        pltpu.make_async_copy(kv_hbm.at[0], kv_ref.at[0], sems.at[0]),
        pltpu.make_async_copy(kv_hbm.at[1], kv_ref.at[1], sems.at[1]),
        pltpu.make_async_copy(w_out_hbm, w_out_ref, sems.at[2]),
    ]
    for copy in copies:
        copy.start()
    owners, peers, cap, width = x_ref.shape
    places = owners * cap
    model = peers * width
    context, slots = kv_ref.shape[1], kv_ref.shape[2]
    group = HD // slots
    steps = (context + group) // group
    for s in range(owners):
        for t in range(peers):
            rows_ref[s * cap : (s + 1) * cap, t * width : (t + 1) * width] = x_ref[s, t]
    wide = rows_ref[...].astype(F32)
    scale = lax.rsqrt(jnp.sum(wide * wide, axis=1, keepdims=True) / model + 1e-05)
    gains = gain_ref[...]
    for k in range(model // HD):
        part = rows_ref[:, k * HD : (k + 1) * HD].astype(F32)
        rows_ref[:, k * HD : (k + 1) * HD] = (part * scale * gains[k : k + 1]).astype(BF)
    normed = rows_ref[...]
    projected = [
        jnp.dot(normed, w_ref[c], preferred_element_type=F32).astype(BF) for c in range(3)
    ]
    collect = collect_ref[...]
    query, new_key, new_value = [
        jnp.dot(collect, p, preferred_element_type=F32).astype(BF) for p in projected
    ]
    lane = lax.broadcasted_iota(jnp.int32, (slots, HD), 1)
    own = lax.broadcasted_iota(jnp.int32, (slots, HD), 0) == lane % slots
    copies[0].wait()
    for g in range(steps):
        if g < steps - 1:
            keys = kv_ref[0, g * group : (g + 1) * group].reshape(HD, HD)
        else:
            tail = kv_ref[0, g * group : context].reshape(HD - slots, HD)
            keys = jnp.concatenate([tail, new_key], axis=0)
        dots = lax.dot_general(
            query, keys, (((1,), (1,)), ((), ())), preferred_element_type=F32
        )
        score_ref[g : g + 1, :] = jnp.sum(jnp.where(own, dots, 0.0), axis=0, keepdims=True)
    scores = score_ref[0:steps, :] * (1.0 / jnp.sqrt(F32(HD)))
    lanes = lax.broadcasted_iota(jnp.int32, (steps, HD), 1)
    frame = lax.broadcasted_iota(jnp.int32, (steps, HD), 0) * group + lanes // slots
    valid = (frame < length_ref[...]) | (frame == context)
    scores = jnp.where(valid, scores, -jnp.inf)
    top = jnp.max(scores, axis=0, keepdims=True)
    shift = slots
    while shift < HD:
        top = jnp.maximum(top, pltpu.roll(top, shift, 1))
        shift *= 2
    expo = jnp.where(valid, jnp.exp(scores - top), 0.0)
    total = jnp.sum(expo, axis=0, keepdims=True)
    shift = slots
    while shift < HD:
        total = total + pltpu.roll(total, shift, 1)
        shift *= 2
    score_ref[0:steps, :] = expo / total
    place = place_ref[...] > 0.0
    copies[1].wait()
    mixed = jnp.zeros((places, HD), F32)
    for g in range(steps):
        weights = jnp.where(place, score_ref[g : g + 1, :], 0.0).astype(BF)
        if g < steps - 1:
            values = kv_ref[1, g * group : (g + 1) * group].reshape(HD, HD)
        else:
            tail = kv_ref[1, g * group : context].reshape(HD - slots, HD)
            values = jnp.concatenate([tail, new_value], axis=0)
        mixed += jnp.dot(weights, values, preferred_element_type=F32)
    attended = mixed.astype(BF)
    copies[2].wait()
    for t in range(peers):
        part = jnp.dot(
            attended, w_out_ref[:, t * width : (t + 1) * width], preferred_element_type=F32
        ).astype(BF)
        for s in range(owners):
            out_ref[s, t] = part[s * cap : (s + 1) * cap]


def finish_kernel(block_ref, session_ref, owner_ref, parts_ref, frames_ref, out_ref, held, sums, count_ref):
    rows = frames_ref.shape[0]
    owners, peers, cap, width = parts_ref.shape
    targets = row_targets(session_ref, owner_ref, block_ref[0], rows, cap, count_ref, owners)
    for o in range(owners):
        held[o * cap : (o + 1) * cap, :] = jnp.sum(parts_ref[o].astype(F32), axis=0)
    for r in range(rows):
        sums[r : r + 1, :] = held[pl.ds(targets[r], 1), :]
    out_ref[...] = (frames_ref[...].astype(F32) + sums[...]).astype(BF)


def body(frames, norm_gain, w_qkv, w_out, kv_cache, frame_session, owner_of, context_len):
    owners = lax.axis_size("sess")
    peers = lax.axis_size("tp")
    rows, width = frames.shape
    slots = kv_cache.shape[1]
    cap = (slots + owners - 1) // owners
    places = owners * cap
    block = lax.axis_index("sess").reshape(1).astype(jnp.int32)
    exchange = (owners, peers, cap, width)

    outgoing = pl.pallas_call(
        dispatch_kernel,
        out_shape=jax.ShapeDtypeStruct(exchange, BF),
        in_specs=[SM, SM, SM, VM],
        out_specs=VM,
        scratch_shapes=[pltpu.VMEM((places, width), F32), pltpu.SMEM((owners,), jnp.int32)],
        name="dispatch",
    )(block, frame_session, owner_of, frames)
    arrived = lax.all_to_all(
        outgoing.reshape(owners * peers, cap, width),
        ("sess", "tp"), split_axis=0, concat_axis=0, tiled=True,
    ).reshape(exchange)

    tables = pl.pallas_call(
        functools.partial(table_kernel, owners),
        out_shape=(
            pltpu.VMEM((slots, places), BF),
            pltpu.VMEM((places, HD), F32),
            pltpu.VMEM((1, HD), jnp.int32),
            pltpu.VMEM((norm_gain.size // HD, HD), F32),
        ),
        in_specs=[SM, VM, VM, VM, VM],
        out_specs=(VM, VM, VM, VM),
        compiler_params=pltpu.CompilerParams(vmem_limit_bytes=4 << 20),
        cost_estimate=pl.CostEstimate(flops=10**9, bytes_accessed=10**6, transcendentals=0),
        name="tables",
    )(block, *[a.reshape(1, -1) for a in (frame_session, owner_of, context_len)], norm_gain.reshape(-1, HD))

    cache = kv_cache.transpose(0, 2, 1, 3)
    context = cache.shape[1]
    steps = (context + HD // slots) // (HD // slots)
    partial_rows = pl.pallas_call(
        attend_kernel,
        out_shape=pltpu.VMEM(exchange, BF),
        in_specs=[VM] * 6 + [pl.BlockSpec(memory_space=pltpu.HBM)] * 2,
        out_specs=VM,
        scratch_shapes=[
            pltpu.VMEM(cache.shape, BF),
            pltpu.VMEM(w_out.shape, BF),
            pltpu.SemaphoreType.DMA((3,)),
            pltpu.VMEM((places, peers * width), BF),
            pltpu.VMEM((steps + (-steps) % 8, HD), F32),
        ],
        name="attend",
        compiler_params=pltpu.CompilerParams(vmem_limit_bytes=10 << 20),
    )(
        *near(arrived, w_qkv, *tables),
        *[pltpu.with_memory_space_constraint(a, pltpu.HBM) for a in (cache, w_out)],
    )
    parts = lax.all_to_all(
        partial_rows.reshape(owners * peers, cap, width),
        ("sess", "tp"), split_axis=0, concat_axis=0, tiled=True,
    ).reshape(exchange)
    return pl.pallas_call(
        finish_kernel,
        out_shape=jax.ShapeDtypeStruct(frames.shape, frames.dtype),
        in_specs=[SM, SM, SM, VM, VM],
        out_specs=VM,
        scratch_shapes=[
            pltpu.VMEM((places, width), F32),
            pltpu.VMEM((rows, width), F32),
            pltpu.SMEM((owners,), jnp.int32),
        ],
        name="finish",
        compiler_params=pltpu.CompilerParams(vmem_limit_bytes=4 << 20),
    )(block, frame_session, owner_of, *near(parts, frames))


def solution(mesh):
    in_specs = (
        P("sess", "tp"),
        P(),
        P(None, None, "tp"),
        P("tp", None),
        P(None, "sess", None, "tp"),
        P(),
        P(),
        P(),
    )
    out_specs = P("sess", "tp")
    return jax.shard_map(body, mesh=mesh, in_specs=in_specs, out_specs=out_specs, check_vma=False)
```

```python
import functools

import jax
import jax.numpy as jnp
from jax import lax
from jax.experimental import pallas as pl
from jax.experimental.pallas import tpu as pltpu
from jax.sharding import PartitionSpec as P

HD = 128
BF = jnp.bfloat16
F32 = jnp.float32
I32 = jnp.int32
VM = pl.BlockSpec(memory_space=pltpu.VMEM)
HBM = pl.BlockSpec(memory_space=pltpu.HBM)


def near(*arrays):
    return [pltpu.with_memory_space_constraint(a, pltpu.VMEM) for a in arrays]


def far(*arrays):
    return [pltpu.with_memory_space_constraint(a, pltpu.HBM) for a in arrays]


def limit(mib):
    return pltpu.CompilerParams(vmem_limit_bytes=mib << 20)


def iota(shape, dim):
    return lax.broadcasted_iota(I32, shape, dim)


def dispatch_kernel(
    owners, cap, session_hbm, owner_hbm, frames_hbm, out_hbm,
    session_ref, owner_ref, frames_ref, held, out_ref, count_ref, in_sems, out_sem,
):
    copies = [
        pltpu.make_async_copy(session_hbm, session_ref, in_sems.at[0]),
        pltpu.make_async_copy(owner_hbm, owner_ref, in_sems.at[1]),
        pltpu.make_async_copy(frames_hbm, frames_ref, in_sems.at[2]),
    ]
    for copy in copies:
        copy.start()
    rows, width = frames_ref.shape
    pieces = width // HD
    chunk = cap * pieces
    held[...] = jnp.zeros_like(held)
    for o in range(owners):
        count_ref[o] = 0
    for copy in copies:
        copy.wait()
    first = lax.axis_index("sess") * rows
    wide = frames_ref[...].astype(F32)
    for r in range(rows):
        o = owner_ref[session_ref[first + r]]
        pair = count_ref[o]
        count_ref[o] = pair + 1
        for f in range(pieces):
            held[pl.ds(o * chunk + pair * pieces + f, 1), :] = wide[r : r + 1, f * HD : (f + 1) * HD]
    span = out_ref.shape[0] // owners
    for o in range(owners):
        piece = held[o * chunk : (o + 1) * chunk, :]
        tile = jnp.concatenate([piece] * (16 // chunk), axis=0).astype(BF)
        for k in range(span // 16):
            out_ref[o * span + k * 16 : o * span + (k + 1) * 16, :] = tile
    copy = pltpu.make_async_copy(out_ref, out_hbm, out_sem)
    copy.start()
    copy.wait()


def table_kernel(
    blocks, session_ref, owner_ref, length_ref, gain_ref,
    collect_ref, place_ref, lane_length_ref, wide_gain_ref, target_ref,
):
    wide_gain_ref[...] = gain_ref[...].astype(F32)
    sessions = session_ref.shape[1]
    slots, places = collect_ref.shape
    me = lax.axis_index("sess")

    def dot(a, b, dims):
        return lax.dot_general(
            a.astype(BF), b.astype(BF), (dims, ((), ())), preferred_element_type=F32
        )

    def one(flag):
        return jnp.where(flag, 1.0, 0.0)

    square = (sessions, sessions)
    before, after = iota(square, 0), iota(square, 1)
    owner_row = jnp.broadcast_to(owner_ref[...], (8, sessions))
    mine = one(owner_row == me)
    slot_of = dot(mine, one(before < after), ((1,), (0,)))
    rows = sessions // blocks
    matches = one(before == session_ref[...])
    row_mine = dot(mine, matches, ((1,), (0,)))
    row_slot = dot(slot_of, matches, ((1,), (0,)))[0:1].astype(I32)
    row_owner = dot(owner_row.astype(F32), matches, ((1,), (0,)))[0:1].astype(I32)
    same_block = (before // rows == after // rows) & (before < after)
    row_pair = dot(row_mine, one(same_block), ((1,), (0,)))[0:1].astype(I32)
    owned = row_mine[0:1] > 0.5
    row_place = row_pair * blocks + iota((1, sessions), 1) // rows
    at_place = (iota((places, sessions), 0) == row_place) & owned
    at_slot = (iota((slots, sessions), 0) == row_slot) & owned
    collect_ref[...] = dot(one(at_slot), one(at_place), ((1,), (1,))).astype(BF)
    place_slot = jnp.sum(jnp.where(at_place, row_slot + 1, 0), axis=1, keepdims=True) - 1
    place_ref[...] = one(place_slot == iota((places, HD), 1) % slots)
    lane_session = one(
        (iota((HD, sessions), 0) % slots == slot_of[0:1].astype(I32)) & (mine[0:1] > 0.5)
    )
    length = jnp.broadcast_to(length_ref[...], (8, sessions))
    high = dot((length >> 4).astype(F32), lane_session, ((1,), (1,)))
    low = dot((length & 15).astype(F32), lane_session, ((1,), (1,)))
    lane_length_ref[...] = (high * 16.0 + low)[0:1].astype(I32)
    local = (rows, sessions)
    row_id = iota(local, 1)
    own_id = me * rows + iota(local, 0)
    own_owner = jnp.sum(jnp.where(row_id == own_id, row_owner, 0), axis=1, keepdims=True)
    earlier = (row_id // rows == me) & (row_id < own_id) & (row_owner == own_owner)
    own_pair = jnp.sum(jnp.where(earlier, 1, 0), axis=1, keepdims=True)
    target_ref[...] = jnp.broadcast_to(own_pair * blocks + own_owner, target_ref.shape)


def turn(tiles):
    row = iota(tiles[0].shape, 0)
    for bit in (4, 2, 1):
        low = (row & bit) == 0
        turned = list(tiles)
        for v in range(8):
            if v & bit == 0:
                a, b = tiles[v], tiles[v + bit]
                turned[v] = jnp.where(low, a, pltpu.roll(b, bit, 0))
                turned[v + bit] = jnp.where(low, pltpu.roll(a, 8 - bit, 0), b)
        tiles = turned
    return tiles


def attend_kernel(
    owners, cap, pieces, x_ref, w_ref, collect_ref, place_ref, length_ref, gain_ref,
    kv_hbm, w_out_hbm, out_ref, kv_ref, w_out_ref, sems, exch_ref, rows_ref, score_ref,
):
    copies = [
        pltpu.make_async_copy(kv_hbm.at[0], kv_ref.at[0], sems.at[0]),
        pltpu.make_async_copy(kv_hbm.at[1], kv_ref.at[1], sems.at[1]),
        pltpu.make_async_copy(w_out_hbm, w_out_ref, sems.at[2]),
    ]
    for copy in copies:
        copy.start()
    places, model = rows_ref.shape
    span = x_ref.shape[0] // owners
    chunk = cap * pieces
    tiles = model // HD
    context, slots = kv_ref.shape[1], kv_ref.shape[2]
    group = HD // slots
    steps = (context + group) // group
    half = steps // 2

    block = 16 // chunk

    def unpack(i, carry):
        for h in range(owners // 8):
            parts = []
            for o in range(8):
                at = pl.multiple_of((h * 8 + o) * span + i * 16, 16)
                parts.append(x_ref[pl.ds(at, 16), :].astype(F32))
            for b in range(2):
                turned = turn([part[b * 8 : (b + 1) * 8] for part in parts])
                for v, tile in enumerate(turned):
                    row = b * 8 + v
                    t, j, f = row // chunk, row % chunk // pieces, row % pieces
                    k = (i * block + t) * pieces + f
                    exch_ref[k, j * owners + h * 8 : j * owners + h * 8 + 8, :] = tile
        return carry

    lax.fori_loop(0, span // 16, unpack, 0)

    squares = [jnp.zeros((places, HD), F32) for _ in range(2)]
    for k in range(tiles):
        part = exch_ref[k]
        squares[k % 2] += part * part
    scale = lax.rsqrt(jnp.sum(squares[0] + squares[1], axis=1, keepdims=True) / model + 1e-05)
    for k in range(tiles):
        cols = slice(k * HD, (k + 1) * HD)
        rows_ref[:, cols] = (exch_ref[k] * scale * gain_ref[k : k + 1, :]).astype(BF)

    deep = 2 * HD
    sums = [jnp.zeros((places, deep), F32) for _ in range(2)]
    for c in range(model // deep):
        at = slice(c * deep, (c + 1) * deep)
        both = jnp.concatenate([w_ref[0, at, :], w_ref[1, at, :]], axis=1)
        sums[c % 2] += jnp.dot(rows_ref[:, at], both, preferred_element_type=F32)
    query_key = (sums[0] + sums[1]).astype(BF)
    sums = [jnp.zeros((2 * places, deep), F32) for _ in range(2)]
    for c in range(model // deep // 2):
        low = slice(c * deep, (c + 1) * deep)
        high = slice(model // 2 + c * deep, model // 2 + (c + 1) * deep)
        both = jnp.concatenate([w_ref[2, low, :], w_ref[2, high, :]], axis=1)
        stacked = jnp.concatenate([rows_ref[:, low], rows_ref[:, high]], axis=0)
        sums[c % 2] += jnp.dot(stacked, both, preferred_element_type=F32)
    total = sums[0] + sums[1]
    value = (total[:places, :HD] + total[places:, HD:]).astype(BF)
    collect = collect_ref[...]
    query_key = jnp.dot(collect, query_key, preferred_element_type=F32).astype(BF)
    query, new_key = query_key[:, :HD], query_key[:, HD:]
    new_value = jnp.dot(collect, value, preferred_element_type=F32).astype(BF)

    own = iota((slots, HD), 0) == iota((slots, HD), 1) % slots
    copies[0].wait()
    for g in range(half):
        first = 2 * g * group
        last = min(first + 2 * group, context)
        keys = kv_ref[0, first:last].reshape((last - first) * slots, HD)
        if last - first < 2 * group:
            keys = jnp.concatenate([keys, new_key], axis=0)
        dots = lax.dot_general(
            query, keys, (((1,), (1,)), ((), ())), preferred_element_type=F32
        )
        for i in range(2):
            part = jnp.where(own, dots[:, i * HD : (i + 1) * HD], 0.0)
            score_ref[2 * g + i : 2 * g + i + 1, :] = jnp.sum(part, axis=0, keepdims=True)
    scores = score_ref[0:steps, :] * (1.0 / jnp.sqrt(F32(HD)))
    frame = iota((steps, HD), 0) * group + iota((steps, HD), 1) // slots
    valid = (frame < length_ref[...]) | (frame == context)
    scores = jnp.where(valid, scores, -jnp.inf)
    top = jnp.max(scores, axis=0, keepdims=True)
    shift = slots
    while shift < HD:
        top = jnp.maximum(top, pltpu.roll(top, shift, 1))
        shift *= 2
    expo = jnp.where(valid, jnp.exp(scores - top), 0.0)
    total = jnp.sum(expo, axis=0, keepdims=True)
    shift = slots
    while shift < HD:
        total = total + pltpu.roll(total, shift, 1)
        shift *= 2
    score_ref[0:steps, :] = expo / total

    place = place_ref[...] > 0.0

    def weights(step):
        return jnp.where(place, score_ref[step : step + 1, :], 0.0).astype(BF)

    def values(step, count):
        first = step * group
        last = min(first + count * group, context)
        found = kv_ref[1, first:last].reshape((last - first) * slots, HD)
        if last - first < count * group:
            found = jnp.concatenate([found, new_value], axis=0)
        return found

    copies[1].wait()
    sums = [jnp.zeros((2 * places, deep), F32) for _ in range(2)]
    for c in range((half + 1) // 2):
        count = min(2, half - 2 * c)
        left, right = 2 * c, half + 2 * c
        stacked = jnp.concatenate(
            [
                jnp.concatenate([weights(at + i) for i in range(count)], axis=1)
                for at in (left, right)
            ],
            axis=0,
        )
        both = jnp.concatenate([values(left, count), values(right, count)], axis=1)
        sums[c % 2] += jnp.dot(stacked, both, preferred_element_type=F32)
    total = sums[0] + sums[1]
    attended = (total[:places, :HD] + total[places:, HD:]).astype(BF)
    copies[2].wait()
    width = pieces * HD
    for i in range(span // 16):
        found = [
            jnp.dot(
                attended,
                w_out_ref[:, (i * block + t) * width : (i * block + t + 1) * width],
                preferred_element_type=F32,
            )
            for t in range(block)
        ]
        for h in range(owners // 8):
            turned = []
            for b in range(2):
                tiles_in = []
                for v in range(8):
                    row = b * 8 + v
                    t, j, f = row // chunk, row % chunk // pieces, row % pieces
                    first = j * owners + h * 8
                    tiles_in.append(found[t][first : first + 8, f * HD : (f + 1) * HD])
                turned.append(turn(tiles_in))
            for o in range(8):
                at = (h * 8 + o) * span + i * 16
                both = jnp.concatenate([turned[0][o], turned[1][o]], axis=0)
                out_ref[at : at + 16, :] = both.astype(BF)


def finish_kernel(owners, cap, parts_ref, frames_ref, target_ref, out_ref, sums_ref):
    rows, width = frames_ref.shape
    pieces = width // HD
    chunk = cap * pieces
    span = parts_ref.shape[0] // owners
    for o in range(owners):
        part = parts_ref[o * span : (o + 1) * span, :].astype(F32)
        part = jnp.sum(part.reshape(span // 8, 8, HD), axis=0)
        shift = chunk
        while shift < 8:
            part = part + pltpu.roll(part, shift, 0)
            shift *= 2
        sums_ref[o * chunk : (o + 1) * chunk, :] = part[:chunk]
    target = target_ref[...]
    found = [jnp.zeros((rows, HD), F32) for _ in range(pieces)]
    for o in range(owners):
        for j in range(cap):
            here = target == j * owners + o
            for f in range(pieces):
                at = o * chunk + j * pieces + f
                found[f] = jnp.where(here, sums_ref[at : at + 1, :], found[f])
    for f in range(pieces):
        cols = slice(f * HD, (f + 1) * HD)
        out_ref[:, cols] = (frames_ref[:, cols].astype(F32) + found[f]).astype(BF)


def exchanged(array):
    return lax.all_to_all(array, ("sess", "tp"), split_axis=0, concat_axis=0, tiled=True)


def body(frames, norm_gain, w_qkv, w_out, kv_cache, frame_session, owner_of, context_len):
    owners = lax.axis_size("sess")
    peers = lax.axis_size("tp")
    rows, width = frames.shape
    slots = kv_cache.shape[1]
    cap = (slots + owners - 1) // owners
    places = owners * cap
    pieces = width // HD
    exchange = (owners * peers * cap * pieces, HD)

    outgoing = pl.pallas_call(
        functools.partial(dispatch_kernel, owners, cap),
        out_shape=pltpu.HBM(exchange, BF),
        in_specs=[HBM, HBM, HBM],
        out_specs=HBM,
        scratch_shapes=[
            pltpu.SMEM(frame_session.shape, I32),
            pltpu.SMEM(owner_of.shape, I32),
            pltpu.VMEM(frames.shape, BF),
            pltpu.VMEM((places * pieces, HD), F32),
            pltpu.VMEM(exchange, BF),
            pltpu.SMEM((owners,), I32),
            pltpu.SemaphoreType.DMA((3,)),
            pltpu.SemaphoreType.DMA,
        ],
        compiler_params=limit(4),
        name="dispatch",
    )(*far(frame_session, owner_of, frames))
    arrived = exchanged(outgoing)

    tables = pl.pallas_call(
        functools.partial(table_kernel, owners),
        out_shape=(
            pltpu.VMEM((slots, places), BF),
            pltpu.VMEM((places, HD), F32),
            pltpu.VMEM((1, HD), I32),
            pltpu.VMEM((norm_gain.size // HD, HD), F32),
            pltpu.VMEM((rows, HD), I32),
        ),
        in_specs=[VM] * 4,
        out_specs=(VM,) * 5,
        compiler_params=limit(4),
        cost_estimate=pl.CostEstimate(flops=10**9, bytes_accessed=10**6, transcendentals=0),
        name="tables",
    )(
        *[a.reshape(1, -1) for a in (frame_session, owner_of, context_len)],
        norm_gain.reshape(-1, HD),
    )
    *tables, target = tables

    cache = kv_cache.transpose(0, 2, 1, 3)
    steps = (cache.shape[1] + HD // slots) // (HD // slots)
    partial_rows = pl.pallas_call(
        functools.partial(attend_kernel, owners, cap, pieces),
        out_shape=pltpu.VMEM(exchange, BF),
        in_specs=[VM] * 6 + [HBM, HBM],
        out_specs=VM,
        scratch_shapes=[
            pltpu.VMEM(cache.shape, BF),
            pltpu.VMEM(w_out.shape, BF),
            pltpu.SemaphoreType.DMA((3,)),
            pltpu.VMEM((peers * pieces, places, HD), F32),
            pltpu.VMEM((places, peers * width), BF),
            pltpu.VMEM((steps + (-steps) % 8, HD), F32),
        ],
        compiler_params=limit(10),
        name="attend",
    )(*near(arrived, w_qkv, *tables), *far(cache, w_out))
    parts = exchanged(partial_rows)
    return pl.pallas_call(
        functools.partial(finish_kernel, owners, cap),
        out_shape=jax.ShapeDtypeStruct(frames.shape, frames.dtype),
        in_specs=[VM] * 3,
        out_specs=VM,
        scratch_shapes=[pltpu.VMEM((places * pieces, HD), F32)],
        compiler_params=limit(4),
        name="finish",
    )(*near(parts, frames, target))


def solution(mesh):
    in_specs = (
        P("sess", "tp"),
        P(),
        P(None, None, "tp"),
        P("tp", None),
        P(None, "sess", None, "tp"),
        P(),
        P(),
        P(),
    )
    out_specs = P("sess", "tp")
    return jax.shard_map(body, mesh=mesh, in_specs=in_specs, out_specs=out_specs, check_vma=False)
```

```python
import functools

import jax
import jax.numpy as jnp
from jax import lax
from jax.experimental import pallas as pl
from jax.experimental.pallas import tpu as pltpu
from jax.sharding import PartitionSpec as P

HD = 128
BF = jnp.bfloat16
F32 = jnp.float32
I32 = jnp.int32
VM = pl.BlockSpec(memory_space=pltpu.VMEM)
HBM = pl.BlockSpec(memory_space=pltpu.HBM)


def near(*arrays):
    return [pltpu.with_memory_space_constraint(a, pltpu.VMEM) for a in arrays]


def far(*arrays):
    return [pltpu.with_memory_space_constraint(a, pltpu.HBM) for a in arrays]


def limit(mib):
    return pltpu.CompilerParams(vmem_limit_bytes=mib << 20)


def iota(shape, dim):
    return lax.broadcasted_iota(I32, shape, dim)


def dispatch_kernel(
    owners, cap, session_hbm, owner_hbm, frames_hbm, out_hbm,
    session_ref, owner_ref, frames_ref, held, out_ref, count_ref, in_sems, out_sem,
):
    copies = [
        pltpu.make_async_copy(session_hbm, session_ref, in_sems.at[0]),
        pltpu.make_async_copy(owner_hbm, owner_ref, in_sems.at[1]),
        pltpu.make_async_copy(frames_hbm, frames_ref, in_sems.at[2]),
    ]
    for copy in copies:
        copy.start()
    rows, width = frames_ref.shape
    pieces = width // HD
    chunk = cap * pieces
    held[...] = jnp.zeros_like(held)
    for o in range(owners):
        count_ref[o] = 0
    for copy in copies:
        copy.wait()
    first = lax.axis_index("sess") * rows
    wide = frames_ref[...].astype(F32)
    for r in range(rows):
        o = owner_ref[session_ref[first + r]]
        pair = count_ref[o]
        count_ref[o] = pair + 1
        for f in range(pieces):
            held[pl.ds(o * chunk + pair * pieces + f, 1), :] = wide[r : r + 1, f * HD : (f + 1) * HD]
    span = out_ref.shape[0] // owners
    for o in range(owners):
        piece = held[o * chunk : (o + 1) * chunk, :]
        tile = jnp.concatenate([piece] * (16 // chunk), axis=0).astype(BF)
        for k in range(span // 16):
            out_ref[o * span + k * 16 : o * span + (k + 1) * 16, :] = tile
    copy = pltpu.make_async_copy(out_ref, out_hbm, out_sem)
    copy.start()
    copy.wait()


def table_kernel(
    blocks, session_ref, owner_ref, length_ref, gain_ref,
    collect_ref, place_ref, lane_length_ref, wide_gain_ref, target_ref,
):
    wide_gain_ref[...] = gain_ref[...].astype(F32)
    sessions = session_ref.shape[1]
    slots, places = collect_ref.shape
    me = lax.axis_index("sess")

    def dot(a, b, dims):
        return lax.dot_general(
            a.astype(BF), b.astype(BF), (dims, ((), ())), preferred_element_type=F32
        )

    def one(flag):
        return jnp.where(flag, 1.0, 0.0)

    square = (sessions, sessions)
    before, after = iota(square, 0), iota(square, 1)
    owner_row = jnp.broadcast_to(owner_ref[...], (8, sessions))
    mine = one(owner_row == me)
    slot_of = dot(mine, one(before < after), ((1,), (0,)))
    rows = sessions // blocks
    matches = one(before == session_ref[...])
    row_mine = dot(mine, matches, ((1,), (0,)))
    row_slot = dot(slot_of, matches, ((1,), (0,)))[0:1].astype(I32)
    row_owner = dot(owner_row.astype(F32), matches, ((1,), (0,)))[0:1].astype(I32)
    same_block = (before // rows == after // rows) & (before < after)
    row_pair = dot(row_mine, one(same_block), ((1,), (0,)))[0:1].astype(I32)
    owned = row_mine[0:1] > 0.5
    row_place = row_pair * blocks + iota((1, sessions), 1) // rows
    at_place = (iota((places, sessions), 0) == row_place) & owned
    at_slot = (iota((slots, sessions), 0) == row_slot) & owned
    collect_ref[...] = dot(one(at_slot), one(at_place), ((1,), (1,))).astype(BF)
    place_slot = jnp.sum(jnp.where(at_place, row_slot + 1, 0), axis=1, keepdims=True) - 1
    place_ref[...] = one(place_slot == iota((places, HD), 1) % slots)
    lane_session = one(
        (iota((HD, sessions), 0) % slots == slot_of[0:1].astype(I32)) & (mine[0:1] > 0.5)
    )
    length = jnp.broadcast_to(length_ref[...], (8, sessions))
    high = dot((length >> 4).astype(F32), lane_session, ((1,), (1,)))
    low = dot((length & 15).astype(F32), lane_session, ((1,), (1,)))
    lane_length_ref[...] = (high * 16.0 + low)[0:1].astype(I32)
    local = (rows, sessions)
    row_id = iota(local, 1)
    own_id = me * rows + iota(local, 0)
    own_owner = jnp.sum(jnp.where(row_id == own_id, row_owner, 0), axis=1, keepdims=True)
    earlier = (row_id // rows == me) & (row_id < own_id) & (row_owner == own_owner)
    own_pair = jnp.sum(jnp.where(earlier, 1, 0), axis=1, keepdims=True)
    target_ref[...] = jnp.broadcast_to(own_pair * blocks + own_owner, target_ref.shape)


def turn(tiles):
    row = iota(tiles[0].shape, 0)
    for bit in (4, 2, 1):
        low = (row & bit) == 0
        turned = list(tiles)
        for v in range(8):
            if v & bit == 0:
                a, b = tiles[v], tiles[v + bit]
                turned[v] = jnp.where(low, a, pltpu.roll(b, bit, 0))
                turned[v + bit] = jnp.where(low, pltpu.roll(a, 8 - bit, 0), b)
        tiles = turned
    return tiles


def attend_kernel(
    owners, cap, pieces, x_ref, w_ref, collect_ref, place_ref, length_ref, gain_ref,
    kv_hbm, w_out_hbm, out_ref, kv_ref, w_out_ref, sems, exch_ref, rows_ref, score_ref, sum_ref,
):
    copies = [
        pltpu.make_async_copy(kv_hbm.at[0], kv_ref.at[0], sems.at[0]),
        pltpu.make_async_copy(kv_hbm.at[1], kv_ref.at[1], sems.at[1]),
        pltpu.make_async_copy(w_out_hbm, w_out_ref, sems.at[2]),
    ]
    for copy in copies:
        copy.start()
    places, model = rows_ref.shape
    span = x_ref.shape[0] // owners
    chunk = cap * pieces
    tiles = model // HD
    context, slots = kv_ref.shape[1], kv_ref.shape[2]
    group = HD // slots
    steps = (context + group) // group
    half = steps // 2

    block = 16 // chunk

    def unpack(i, carry):
        for h in range(owners // 8):
            parts = []
            for o in range(8):
                at = pl.multiple_of((h * 8 + o) * span + i * 16, 16)
                parts.append(x_ref[pl.ds(at, 16), :].astype(F32))
            for b in range(2):
                turned = turn([part[b * 8 : (b + 1) * 8] for part in parts])
                for v, tile in enumerate(turned):
                    row = b * 8 + v
                    t, j, f = row // chunk, row % chunk // pieces, row % pieces
                    k = (i * block + t) * pieces + f
                    exch_ref[k, j * owners + h * 8 : j * owners + h * 8 + 8, :] = tile
        return carry

    lax.fori_loop(0, span // 16, unpack, 0)

    squares = [jnp.zeros((places, HD), F32) for _ in range(2)]
    for k in range(tiles):
        part = exch_ref[k]
        squares[k % 2] += part * part
    scale = lax.rsqrt(jnp.sum(squares[0] + squares[1], axis=1, keepdims=True) / model + 1e-05)
    for k in range(tiles):
        cols = slice(k * HD, (k + 1) * HD)
        rows_ref[:, cols] = (exch_ref[k] * scale * gain_ref[k : k + 1, :]).astype(BF)

    deep = 2 * HD
    sums = [jnp.zeros((places, deep), F32) for _ in range(2)]
    for c in range(model // deep):
        at = slice(c * deep, (c + 1) * deep)
        both = jnp.concatenate([w_ref[0, at, :], w_ref[1, at, :]], axis=1)
        sums[c % 2] += jnp.dot(rows_ref[:, at], both, preferred_element_type=F32)
    for i in range(2):
        sum_ref[i, :places] = sums[i]
    sums = [jnp.zeros((2 * places, deep), F32) for _ in range(2)]
    for c in range(model // deep // 2):
        low = slice(c * deep, (c + 1) * deep)
        high = slice(model // 2 + c * deep, model // 2 + (c + 1) * deep)
        both = jnp.concatenate([w_ref[2, low, :], w_ref[2, high, :]], axis=1)
        stacked = jnp.concatenate([rows_ref[:, low], rows_ref[:, high]], axis=0)
        sums[c % 2] += jnp.dot(stacked, both, preferred_element_type=F32)
    for i in range(2):
        sum_ref[2 + i] = sums[i]
    live = lax.axis_index("sess") >= 0

    @pl.when(live)
    def _():
        query_key = (sum_ref[0, :places] + sum_ref[1, :places]).astype(BF)
        total = sum_ref[2] + sum_ref[3]
        value = (total[:places, :HD] + total[places:, HD:]).astype(BF)
        collect = collect_ref[...]
        query_key = jnp.dot(collect, query_key, preferred_element_type=F32).astype(BF)
        query, new_key = query_key[:, :HD], query_key[:, HD:]
        new_value = jnp.dot(collect, value, preferred_element_type=F32).astype(BF)

        own = iota((slots, HD), 0) == iota((slots, HD), 1) % slots
        copies[0].wait()
        for g in range(half):
            first = 2 * g * group
            last = min(first + 2 * group, context)
            keys = kv_ref[0, first:last].reshape((last - first) * slots, HD)
            if last - first < 2 * group:
                keys = jnp.concatenate([keys, new_key], axis=0)
            dots = lax.dot_general(
                query, keys, (((1,), (1,)), ((), ())), preferred_element_type=F32
            )
            for i in range(2):
                part = jnp.where(own, dots[:, i * HD : (i + 1) * HD], 0.0)
                score_ref[2 * g + i : 2 * g + i + 1, :] = jnp.sum(part, axis=0, keepdims=True)
        scores = score_ref[0:steps, :] * (1.0 / jnp.sqrt(F32(HD)))
        frame = iota((steps, HD), 0) * group + iota((steps, HD), 1) // slots
        valid = (frame < length_ref[...]) | (frame == context)
        scores = jnp.where(valid, scores, -jnp.inf)
        top = jnp.max(scores, axis=0, keepdims=True)
        shift = slots
        while shift < HD:
            top = jnp.maximum(top, pltpu.roll(top, shift, 1))
            shift *= 2
        expo = jnp.where(valid, jnp.exp(scores - top), 0.0)
        total = jnp.sum(expo, axis=0, keepdims=True)
        shift = slots
        while shift < HD:
            total = total + pltpu.roll(total, shift, 1)
            shift *= 2
        score_ref[0:steps, :] = expo / total

        place = place_ref[...] > 0.0

        def weights(step):
            return jnp.where(place, score_ref[step : step + 1, :], 0.0).astype(BF)

        def values(step, count):
            first = step * group
            last = min(first + count * group, context)
            found = kv_ref[1, first:last].reshape((last - first) * slots, HD)
            if last - first < count * group:
                found = jnp.concatenate([found, new_value], axis=0)
            return found

        copies[1].wait()
        sums = [jnp.zeros((2 * places, deep), F32) for _ in range(2)]
        for c in range((half + 1) // 2):
            count = min(2, half - 2 * c)
            left, right = 2 * c, half + 2 * c
            stacked = jnp.concatenate(
                [
                    jnp.concatenate([weights(at + i) for i in range(count)], axis=1)
                    for at in (left, right)
                ],
                axis=0,
            )
            both = jnp.concatenate([values(left, count), values(right, count)], axis=1)
            sums[c % 2] += jnp.dot(stacked, both, preferred_element_type=F32)
        for i in range(2):
            sum_ref[i] = sums[i]

        @pl.when(live)
        def _():
            total = sum_ref[0] + sum_ref[1]
            attended = (total[:places, :HD] + total[places:, HD:]).astype(BF)
            copies[2].wait()
            width = pieces * HD
            for i in range(span // 16):
                found = [
                    jnp.dot(
                        attended,
                        w_out_ref[:, (i * block + t) * width : (i * block + t + 1) * width],
                        preferred_element_type=F32,
                    )
                    for t in range(block)
                ]
                for h in range(owners // 8):
                    turned = []
                    for b in range(2):
                        tiles_in = []
                        for v in range(8):
                            row = b * 8 + v
                            t, j, f = row // chunk, row % chunk // pieces, row % pieces
                            first = j * owners + h * 8
                            tiles_in.append(found[t][first : first + 8, f * HD : (f + 1) * HD])
                        turned.append(turn(tiles_in))
                    for o in range(8):
                        at = (h * 8 + o) * span + i * 16
                        both = jnp.concatenate([turned[0][o], turned[1][o]], axis=0)
                        out_ref[at : at + 16, :] = both.astype(BF)


def finish_kernel(owners, cap, parts_ref, frames_ref, target_ref, out_ref, sums_ref):
    rows, width = frames_ref.shape
    pieces = width // HD
    chunk = cap * pieces
    span = parts_ref.shape[0] // owners
    for o in range(owners):
        part = parts_ref[o * span : (o + 1) * span, :].astype(F32)
        part = jnp.sum(part.reshape(span // 8, 8, HD), axis=0)
        shift = chunk
        while shift < 8:
            part = part + pltpu.roll(part, shift, 0)
            shift *= 2
        sums_ref[o * chunk : (o + 1) * chunk, :] = part[:chunk]
    target = target_ref[...]
    found = [jnp.zeros((rows, HD), F32) for _ in range(pieces)]
    for o in range(owners):
        for j in range(cap):
            here = target == j * owners + o
            for f in range(pieces):
                at = o * chunk + j * pieces + f
                found[f] = jnp.where(here, sums_ref[at : at + 1, :], found[f])
    for f in range(pieces):
        cols = slice(f * HD, (f + 1) * HD)
        out_ref[:, cols] = (frames_ref[:, cols].astype(F32) + found[f]).astype(BF)


def exchanged(array):
    return lax.all_to_all(array, ("sess", "tp"), split_axis=0, concat_axis=0, tiled=True)


def body(frames, norm_gain, w_qkv, w_out, kv_cache, frame_session, owner_of, context_len):
    owners = lax.axis_size("sess")
    peers = lax.axis_size("tp")
    rows, width = frames.shape
    slots = kv_cache.shape[1]
    cap = (slots + owners - 1) // owners
    places = owners * cap
    pieces = width // HD
    exchange = (owners * peers * cap * pieces, HD)

    outgoing = pl.pallas_call(
        functools.partial(dispatch_kernel, owners, cap),
        out_shape=pltpu.HBM(exchange, BF),
        in_specs=[HBM, HBM, HBM],
        out_specs=HBM,
        scratch_shapes=[
            pltpu.SMEM(frame_session.shape, I32),
            pltpu.SMEM(owner_of.shape, I32),
            pltpu.VMEM(frames.shape, BF),
            pltpu.VMEM((places * pieces, HD), F32),
            pltpu.VMEM(exchange, BF),
            pltpu.SMEM((owners,), I32),
            pltpu.SemaphoreType.DMA((3,)),
            pltpu.SemaphoreType.DMA,
        ],
        compiler_params=limit(4),
        name="dispatch",
    )(*far(frame_session, owner_of, frames))
    arrived = exchanged(outgoing)

    tables = pl.pallas_call(
        functools.partial(table_kernel, owners),
        out_shape=(
            pltpu.VMEM((slots, places), BF),
            pltpu.VMEM((places, HD), F32),
            pltpu.VMEM((1, HD), I32),
            pltpu.VMEM((norm_gain.size // HD, HD), F32),
            pltpu.VMEM((rows, HD), I32),
        ),
        in_specs=[VM] * 4,
        out_specs=(VM,) * 5,
        compiler_params=limit(4),
        cost_estimate=pl.CostEstimate(flops=10**9, bytes_accessed=10**6, transcendentals=0),
        name="tables",
    )(
        *[a.reshape(1, -1) for a in (frame_session, owner_of, context_len)],
        norm_gain.reshape(-1, HD),
    )
    *tables, target = tables

    cache = kv_cache.transpose(0, 2, 1, 3)
    steps = (cache.shape[1] + HD // slots) // (HD // slots)
    partial_rows = pl.pallas_call(
        functools.partial(attend_kernel, owners, cap, pieces),
        out_shape=pltpu.VMEM(exchange, BF),
        in_specs=[VM] * 6 + [HBM, HBM],
        out_specs=VM,
        scratch_shapes=[
            pltpu.VMEM(cache.shape, BF),
            pltpu.VMEM(w_out.shape, BF),
            pltpu.SemaphoreType.DMA((3,)),
            pltpu.VMEM((peers * pieces, places, HD), F32),
            pltpu.VMEM((places, peers * width), BF),
            pltpu.VMEM((steps + (-steps) % 8, HD), F32),
            pltpu.VMEM((4, 2 * places, 2 * HD), F32),
        ],
        compiler_params=limit(10),
        name="attend",
    )(*near(arrived, w_qkv, *tables), *far(cache, w_out))
    parts = exchanged(partial_rows)
    return pl.pallas_call(
        functools.partial(finish_kernel, owners, cap),
        out_shape=jax.ShapeDtypeStruct(frames.shape, frames.dtype),
        in_specs=[VM] * 3,
        out_specs=VM,
        scratch_shapes=[pltpu.VMEM((places * pieces, HD), F32)],
        compiler_params=limit(4),
        name="finish",
    )(*near(parts, frames, target))


def solution(mesh):
    in_specs = (
        P("sess", "tp"),
        P(),
        P(None, None, "tp"),
        P("tp", None),
        P(None, "sess", None, "tp"),
        P(),
        P(),
        P(),
    )
    out_specs = P("sess", "tp")
    return jax.shard_map(body, mesh=mesh, in_specs=in_specs, out_specs=out_specs, check_vma=False)
```

```python
import functools

import jax
import jax.numpy as jnp
from jax import lax
from jax.experimental import pallas as pl
from jax.experimental.pallas import tpu as pltpu
from jax.sharding import PartitionSpec as P

HD = 128
KEY_BLOCK = 192
BF = jnp.bfloat16
F32 = jnp.float32
I32 = jnp.int32
VM = pl.BlockSpec(memory_space=pltpu.VMEM)
HBM = pl.BlockSpec(memory_space=pltpu.HBM)


def near(*arrays):
    return [pltpu.with_memory_space_constraint(a, pltpu.VMEM) for a in arrays]


def far(*arrays):
    return [pltpu.with_memory_space_constraint(a, pltpu.HBM) for a in arrays]


def limit(mib):
    return pltpu.CompilerParams(vmem_limit_bytes=mib << 20)


def iota(shape, dim):
    return lax.broadcasted_iota(I32, shape, dim)


def table_kernel(
    chips, cores, cap, session_hbm, owner_hbm, length_hbm, gain_hbm, frames_hbm,
    collect_ref, place_ref, lane_length_ref, wide_gain_ref, target_ref, send_ref, frames_ref,
    session_ref, owner_ref, length_ref, gain_ref, sems,
):
    pairs = (
        (session_hbm, session_ref), (owner_hbm, owner_ref),
        (length_hbm, length_ref), (gain_hbm, gain_ref), (frames_hbm, frames_ref),
    )
    copies = [pltpu.make_async_copy(a, b, sems.at[i]) for i, (a, b) in enumerate(pairs)]
    for copy in copies:
        copy.start()
    for copy in copies:
        copy.wait()
    wide_gain_ref[...] = gain_ref[...].astype(F32)
    sessions = session_ref.shape[1]
    slots, places = collect_ref.shape
    blocks = chips * cores
    chip, core = lax.axis_index("z"), lax.axis_index("core")
    me = chip * cores + core

    def dot(a, b, dims):
        return lax.dot_general(
            a.astype(BF), b.astype(BF), (dims, ((), ())), preferred_element_type=F32
        )

    def one(flag):
        return jnp.where(flag, 1.0, 0.0)

    square = (sessions, sessions)
    before, after = iota(square, 0), iota(square, 1)
    owner_row = jnp.broadcast_to(owner_ref[...], (8, sessions))
    mine = one(owner_row == me)
    slot_of = dot(mine, one(before < after), ((1,), (0,)))
    rows = sessions // blocks
    matches = one(before == session_ref[...])
    row_mine = dot(mine, matches, ((1,), (0,)))
    row_slot = dot(slot_of, matches, ((1,), (0,)))[0:1].astype(I32)
    row_owner = dot(owner_row.astype(F32), matches, ((1,), (0,)))[0:1].astype(I32)
    same_block = (before // rows == after // rows) & (before < after)
    row_pair = dot(row_mine, one(same_block), ((1,), (0,)))[0:1].astype(I32)
    owned = row_mine[0:1] > 0.5
    row_block = iota((1, sessions), 1) // rows
    row_place = row_pair * blocks + row_block % cores * chips + row_block // cores
    at_place = (iota((places, sessions), 0) == row_place) & owned
    at_slot = (iota((slots, sessions), 0) == row_slot) & owned
    collect_ref[...] = dot(one(at_slot), one(at_place), ((1,), (1,))).astype(BF)
    place_slot = jnp.sum(jnp.where(at_place, row_slot + 1, 0), axis=1, keepdims=True) - 1
    place_ref[...] = one(place_slot == iota((places, HD), 1) % slots)
    lane_session = one(
        (iota((HD, sessions), 0) % slots == slot_of[0:1].astype(I32)) & (mine[0:1] > 0.5)
    )
    length = jnp.broadcast_to(length_ref[...], (8, sessions))
    high = dot((length >> 4).astype(F32), lane_session, ((1,), (1,)))
    low = dot((length & 15).astype(F32), lane_session, ((1,), (1,)))
    lane_length_ref[...] = (high * 16.0 + low)[0:1].astype(I32)

    def local(block):
        shape = (rows, sessions)
        row_id = iota(shape, 1)
        own_id = block * rows + iota(shape, 0)
        own_owner = jnp.sum(jnp.where(row_id == own_id, row_owner, 0), axis=1, keepdims=True)
        earlier = (row_id // rows == block) & (row_id < own_id) & (row_owner == own_owner)
        return own_owner, jnp.sum(jnp.where(earlier, 1, 0), axis=1, keepdims=True)

    for side in range(2):
        source = jnp.where(side == 0, core, 1 - core)
        owner, pair = local(chip * cores + source)
        if side == 0:
            target_ref[...] = jnp.broadcast_to(pair * blocks + owner, target_ref.shape)
        line = (owner // cores * cores + source) * cap + pair
        line = jnp.where(owner % cores == core, line, -1)
        lanes = iota((rows, send_ref.shape[1]), 1)
        send_ref[side * rows : (side + 1) * rows, :] = one(lanes == line).astype(BF)


def dispatch_kernel(
    chips, cores, cap, send_ref, frames_ref, other_ref, out_hbm, held, out_ref, sem
):
    rows, width = frames_ref.shape
    pieces = width // HD
    chunk = cores * cap * pieces
    lines = lax.dot_general(
        send_ref[:rows], frames_ref[...], (((0,), (0,)), ((), ())), preferred_element_type=F32
    ) + lax.dot_general(
        send_ref[rows:], other_ref[...], (((0,), (0,)), ((), ())), preferred_element_type=F32
    )
    lines = lines[: chips * cores * cap]
    for f in range(pieces):
        held[pl.ds(f, chips * cores * cap, stride=pieces), :] = lines[:, f * HD : (f + 1) * HD]
    span = out_ref.shape[0] // chips
    for z in range(chips):
        piece = held[z * chunk : (z + 1) * chunk, :]
        tile = jnp.concatenate([piece] * (16 // chunk), axis=0).astype(BF)
        for k in range(span // 16):
            out_ref[z * span + k * 16 : z * span + (k + 1) * 16, :] = tile
    copy = pltpu.make_async_copy(out_ref, out_hbm, sem)
    copy.start()
    copy.wait()


def turn(tiles):
    row = iota(tiles[0].shape, 0)
    for bit in (4, 2, 1):
        low = (row & bit) == 0
        turned = list(tiles)
        for v in range(8):
            if v & bit == 0:
                a, b = tiles[v], tiles[v + bit]
                turned[v] = jnp.where(low, a, pltpu.roll(b, bit, 0))
                turned[v + bit] = jnp.where(low, pltpu.roll(a, 8 - bit, 0), b)
        tiles = turned
    return tiles


def attend_kernel(
    chips, cores, cap, pieces, x_ref, w_ref, collect_ref, place_ref, length_ref, gain_ref,
    kv_hbm, w_out_hbm, out_ref, kv_ref, w_out_ref, sems, exch_ref, rows_ref, score_ref, sum_ref,
):
    key_copies = []
    for i, first in enumerate(range(0, kv_ref.shape[1], KEY_BLOCK)):
        at = pl.ds(first, min(KEY_BLOCK, kv_ref.shape[1] - first))
        key_copies.append(pltpu.make_async_copy(kv_hbm.at[0, at], kv_ref.at[0, at], sems.at[2 + i]))
    copies = [
        pltpu.make_async_copy(kv_hbm.at[1], kv_ref.at[1], sems.at[0]),
        pltpu.make_async_copy(w_out_hbm, w_out_ref, sems.at[1]),
    ]
    for copy in key_copies + copies:
        copy.start()
    places, model = rows_ref.shape
    owners = chips * cores
    tiles = model // HD
    context, slots = kv_ref.shape[1], kv_ref.shape[2]
    group = HD // slots
    steps = (context + group) // group
    half = steps // 2
    span = x_ref.shape[0] // chips
    chunk = cores * cap * pieces

    def unpack(i, carry):
        parts = []
        for z in range(chips):
            at = pl.multiple_of(z * span + i * 16, 16)
            parts.append(x_ref[pl.ds(at, 16), :].astype(F32))
        for b in range(2):
            turned = turn([part[b * 8 : (b + 1) * 8] for part in parts])
            for v, tile in enumerate(turned):
                row = b * 8 + v
                t, line = row // chunk, row % chunk // pieces
                k = (i * (16 // chunk) + t) * pieces + row % pieces
                first = line % cap * owners + line // cap * chips
                exch_ref[k, first : first + chips, :] = tile
        return carry

    lax.fori_loop(0, span // 16, unpack, 0)
    span = out_ref.shape[0] // owners
    chunk = cap * pieces
    block = 16 // chunk

    squares = [jnp.zeros((places, HD), F32) for _ in range(2)]
    for k in range(tiles):
        part = exch_ref[k]
        squares[k % 2] += part * part
    scale = lax.rsqrt(jnp.sum(squares[0] + squares[1], axis=1, keepdims=True) / model + 1e-05)
    for k in range(tiles):
        cols = slice(k * HD, (k + 1) * HD)
        rows_ref[:, cols] = (exch_ref[k] * scale * gain_ref[k : k + 1, :]).astype(BF)

    deep = 2 * HD
    sums = [jnp.zeros((places, deep), F32) for _ in range(2)]
    for c in range(model // deep):
        at = slice(c * deep, (c + 1) * deep)
        both = jnp.concatenate([w_ref[0, at, :], w_ref[1, at, :]], axis=1)
        sums[c % 2] += jnp.dot(rows_ref[:, at], both, preferred_element_type=F32)
    for i in range(2):
        sum_ref[i, :places] = sums[i]
    sums = [jnp.zeros((2 * places, deep), F32) for _ in range(2)]
    for c in range(model // deep // 2):
        low = slice(c * deep, (c + 1) * deep)
        high = slice(model // 2 + c * deep, model // 2 + (c + 1) * deep)
        both = jnp.concatenate([w_ref[2, low, :], w_ref[2, high, :]], axis=1)
        stacked = jnp.concatenate([rows_ref[:, low], rows_ref[:, high]], axis=0)
        sums[c % 2] += jnp.dot(stacked, both, preferred_element_type=F32)
    for i in range(2):
        sum_ref[2 + i] = sums[i]
    live = lax.axis_index("core") >= 0

    @pl.when(live)
    def _():
        query_key = (sum_ref[0, :places] + sum_ref[1, :places]).astype(BF)
        total = sum_ref[2] + sum_ref[3]
        value = (total[:places, :HD] + total[places:, HD:]).astype(BF)
        collect = collect_ref[...]
        query_key = jnp.dot(collect, query_key, preferred_element_type=F32).astype(BF)
        query, new_key = query_key[:, :HD], query_key[:, HD:]
        new_value = jnp.dot(collect, value, preferred_element_type=F32).astype(BF)

        own = iota((slots, HD), 0) == iota((slots, HD), 1) % slots
        for g in range(half):
            first = 2 * g * group
            if first % KEY_BLOCK == 0:
                key_copies[first // KEY_BLOCK].wait()
            last = min(first + 2 * group, context)
            keys = kv_ref[0, first:last].reshape((last - first) * slots, HD)
            if last - first < 2 * group:
                keys = jnp.concatenate([keys, new_key], axis=0)
            dots = lax.dot_general(
                query, keys, (((1,), (1,)), ((), ())), preferred_element_type=F32
            )
            for i in range(2):
                part = jnp.where(own, dots[:, i * HD : (i + 1) * HD], 0.0)
                score_ref[2 * g + i : 2 * g + i + 1, :] = jnp.sum(part, axis=0, keepdims=True)
        scores = score_ref[0:steps, :] * (1.0 / jnp.sqrt(F32(HD)))
        frame = iota((steps, HD), 0) * group + iota((steps, HD), 1) // slots
        valid = (frame < length_ref[...]) | (frame == context)
        scores = jnp.where(valid, scores, -jnp.inf)
        top = jnp.max(scores, axis=0, keepdims=True)
        shift = slots
        while shift < HD:
            top = jnp.maximum(top, pltpu.roll(top, shift, 1))
            shift *= 2
        expo = jnp.where(valid, jnp.exp(scores - top), 0.0)
        total = jnp.sum(expo, axis=0, keepdims=True)
        shift = slots
        while shift < HD:
            total = total + pltpu.roll(total, shift, 1)
            shift *= 2
        score_ref[0:steps, :] = expo / total

        place = place_ref[...] > 0.0

        def weights(step):
            return jnp.where(place, score_ref[step : step + 1, :], 0.0).astype(BF)

        def values(step, count):
            first = step * group
            last = min(first + count * group, context)
            found = kv_ref[1, first:last].reshape((last - first) * slots, HD)
            if last - first < count * group:
                found = jnp.concatenate([found, new_value], axis=0)
            return found

        copies[0].wait()
        sums = [jnp.zeros((2 * places, deep), F32) for _ in range(2)]
        for c in range((half + 1) // 2):
            count = min(2, half - 2 * c)
            left, right = 2 * c, half + 2 * c
            stacked = jnp.concatenate(
                [
                    jnp.concatenate([weights(at + i) for i in range(count)], axis=1)
                    for at in (left, right)
                ],
                axis=0,
            )
            both = jnp.concatenate([values(left, count), values(right, count)], axis=1)
            sums[c % 2] += jnp.dot(stacked, both, preferred_element_type=F32)
        for i in range(2):
            sum_ref[i] = sums[i]

        @pl.when(live)
        def _():
            total = sum_ref[0] + sum_ref[1]
            attended = (total[:places, :HD] + total[places:, HD:]).astype(BF)
            copies[1].wait()
            width = pieces * HD
            for i in range(span // 16):
                found = [
                    jnp.dot(
                        attended,
                        w_out_ref[:, (i * block + t) * width : (i * block + t + 1) * width],
                        preferred_element_type=F32,
                    )
                    for t in range(block)
                ]
                for h in range(cores):
                    turned = []
                    for b in range(2):
                        tiles_in = []
                        for v in range(8):
                            row = b * 8 + v
                            t, j, f = row // chunk, row % chunk // pieces, row % pieces
                            first = j * owners + h * chips
                            tiles_in.append(found[t][first : first + chips, f * HD : (f + 1) * HD])
                        turned.append(turn(tiles_in))
                    for z in range(chips):
                        at = (z * cores + h) * span + i * 16
                        both = jnp.concatenate([turned[0][z], turned[1][z]], axis=0)
                        out_ref[at : at + 16, :] = both.astype(BF)


def attend_scratch(cache, w_out, exchange, tiles, places, model, steps):
    return [
        pltpu.VMEM(cache, BF),
        pltpu.VMEM(w_out, BF),
        pltpu.SemaphoreType.DMA((2 + pl.cdiv(cache[1], KEY_BLOCK),)),
        pltpu.VMEM((tiles, places, HD), F32),
        pltpu.VMEM((places, model), BF),
        pltpu.VMEM((steps + (-steps) % 8, HD), F32),
        pltpu.VMEM((4, 2 * places, 2 * HD), F32),
    ]


def finish_kernel(owners, cap, parts_ref, frames_ref, target_ref, out_ref, sums_ref):
    rows, width = frames_ref.shape
    pieces = width // HD
    chunk = cap * pieces
    span = parts_ref.shape[0] // owners
    for o in range(owners):
        part = parts_ref[o * span : (o + 1) * span, :].astype(F32)
        part = jnp.sum(part.reshape(span // 8, 8, HD), axis=0)
        shift = chunk
        while shift < 8:
            part = part + pltpu.roll(part, shift, 0)
            shift *= 2
        sums_ref[o * chunk : (o + 1) * chunk, :] = part[:chunk]
    target = target_ref[...]
    found = [jnp.zeros((rows, HD), F32) for _ in range(pieces)]
    for o in range(owners):
        for j in range(cap):
            here = target == j * owners + o
            for f in range(pieces):
                at = o * chunk + j * pieces + f
                found[f] = jnp.where(here, sums_ref[at : at + 1, :], found[f])
    for f in range(pieces):
        cols = slice(f * HD, (f + 1) * HD)
        out_ref[:, cols] = (frames_ref[:, cols].astype(F32) + found[f]).astype(BF)


def exchanged(array, axes):
    return lax.all_to_all(array, axes, split_axis=0, concat_axis=0, tiled=True)


def body(frames, norm_gain, w_qkv, w_out, kv_cache, frame_session, owner_of, context_len):
    chips, cores = lax.axis_size("z"), lax.axis_size("core")
    peers = lax.axis_size("tp")
    owners = chips * cores
    rows, width = frames.shape
    slots = kv_cache.shape[1]
    cap = (slots + owners - 1) // owners
    places = owners * cap
    pieces = width // HD
    exchange = (owners * peers * cap * pieces, HD)

    other = lax.ppermute(frames, "core", [(c, c ^ 1) for c in range(cores)])
    lists = [a.reshape(1, -1) for a in (frame_session, owner_of, context_len)]
    gain = norm_gain.reshape(-1, HD)
    *tables, target, send, frames_near = pl.pallas_call(
        functools.partial(table_kernel, chips, cores, cap),
        out_shape=(
            pltpu.VMEM((slots, places), BF),
            pltpu.VMEM((places, HD), F32),
            pltpu.VMEM((1, HD), I32),
            pltpu.VMEM(gain.shape, F32),
            pltpu.VMEM((rows, HD), I32),
            pltpu.VMEM((2 * rows, HD), BF),
            pltpu.VMEM(frames.shape, frames.dtype),
        ),
        in_specs=[HBM] * 5,
        out_specs=(VM,) * 7,
        scratch_shapes=[
            *[pltpu.VMEM(a.shape, a.dtype) for a in (*lists, gain)],
            pltpu.SemaphoreType.DMA((5,)),
        ],
        compiler_params=limit(4),
        cost_estimate=pl.CostEstimate(flops=10**9, bytes_accessed=10**6, transcendentals=0),
        name="tables",
    )(*far(*lists, gain, frames))
    outgoing = pl.pallas_call(
        functools.partial(dispatch_kernel, chips, cores, cap),
        out_shape=pltpu.HBM(exchange, BF),
        in_specs=[VM] * 3,
        out_specs=HBM,
        scratch_shapes=[
            pltpu.VMEM((places * pieces, HD), F32),
            pltpu.VMEM(exchange, BF),
            pltpu.SemaphoreType.DMA,
        ],
        compiler_params=limit(4),
        name="dispatch",
    )(*near(send, frames_near, other))
    arrived = exchanged(outgoing, ("z", "tp"))

    cache = kv_cache.transpose(0, 2, 1, 3)
    steps = (cache.shape[1] + HD // slots) // (HD // slots)
    partial_rows = pl.pallas_call(
        functools.partial(attend_kernel, chips, cores, cap, pieces),
        out_shape=pltpu.VMEM(exchange, BF),
        in_specs=[VM] * 6 + [HBM, HBM],
        out_specs=VM,
        scratch_shapes=attend_scratch(
            cache.shape, w_out.shape, exchange, peers * pieces, places, peers * width, steps
        ),
        compiler_params=limit(10),
        name="attend",
    )(*near(arrived, w_qkv, *tables), *far(cache, w_out))
    parts = exchanged(partial_rows, ("z", "core", "tp"))
    return pl.pallas_call(
        functools.partial(finish_kernel, owners, cap),
        out_shape=jax.ShapeDtypeStruct(frames.shape, frames.dtype),
        in_specs=[VM] * 3,
        out_specs=VM,
        scratch_shapes=[pltpu.VMEM((places * pieces, HD), F32)],
        compiler_params=limit(4),
        name="finish",
    )(*near(parts, frames_near, target))


def solution(mesh):
    sess, tp = mesh.shape["sess"], mesh.shape["tp"]
    split = jax.sharding.Mesh(mesh.devices.reshape(sess // 2, 2, tp), ("z", "core", "tp"))
    owner = ("z", "core")
    in_specs = (
        P(owner, "tp"),
        P(),
        P(None, None, "tp"),
        P("tp", None),
        P(None, owner, None, "tp"),
        P(),
        P(),
        P(),
    )
    out_specs = P(owner, "tp")
    return jax.shard_map(body, mesh=split, in_specs=in_specs, out_specs=out_specs, check_vma=False)
```

```python
import functools

import jax
import jax.numpy as jnp
from jax import lax
from jax.experimental import pallas as pl
from jax.experimental.pallas import tpu as pltpu
from jax.sharding import PartitionSpec as P

HD = 128
KEY_BLOCK = 192
BF = jnp.bfloat16
F32 = jnp.float32
I32 = jnp.int32
VM = pl.BlockSpec(memory_space=pltpu.VMEM)
HBM = pl.BlockSpec(memory_space=pltpu.HBM)


def near(*arrays):
    return [pltpu.with_memory_space_constraint(a, pltpu.VMEM) for a in arrays]


def far(*arrays):
    return [pltpu.with_memory_space_constraint(a, pltpu.HBM) for a in arrays]


def limit(mib):
    return pltpu.CompilerParams(vmem_limit_bytes=mib << 20)


def iota(shape, dim):
    return lax.broadcasted_iota(I32, shape, dim)


def dispatch_kernel(
    owners, cap, session_hbm, owner_hbm, frames_hbm, out_hbm,
    session_ref, owner_ref, frames_ref, held, out_ref, count_ref, in_sems, out_sems,
):
    copies = [
        pltpu.make_async_copy(session_hbm, session_ref, in_sems.at[0]),
        pltpu.make_async_copy(owner_hbm, owner_ref, in_sems.at[1]),
        pltpu.make_async_copy(frames_hbm, frames_ref, in_sems.at[2]),
    ]
    for copy in copies:
        copy.start()
    rows, width = frames_ref.shape
    pieces = width // HD
    chunk = cap * pieces
    held[...] = jnp.zeros_like(held)
    for o in range(owners):
        count_ref[o] = 0
    for copy in copies:
        copy.wait()
    first = lax.axis_index("sess") * rows
    wide = frames_ref[...].astype(F32)
    for r in range(rows):
        o = owner_ref[session_ref[first + r]]
        pair = count_ref[o]
        count_ref[o] = pair + 1
        for f in range(pieces):
            held[pl.ds(o * chunk + pair * pieces + f, 1), :] = wide[r : r + 1, f * HD : (f + 1) * HD]
    span = out_ref.shape[0] // owners
    parts = out_sems.shape[0]
    sent = []
    for o in range(owners):
        piece = held[o * chunk : (o + 1) * chunk, :]
        tile = jnp.concatenate([piece] * (16 // chunk), axis=0).astype(BF)
        for k in range(span // 16):
            out_ref[o * span + k * 16 : o * span + (k + 1) * 16, :] = tile
        if (o + 1) % (owners // parts) == 0:
            at = pl.ds((o + 1 - owners // parts) * span, owners // parts * span)
            copy = pltpu.make_async_copy(out_ref.at[at], out_hbm.at[at], out_sems.at[o // (owners // parts)])
            copy.start()
            sent.append(copy)
    for copy in sent:
        copy.wait()


def table_kernel(
    blocks, session_ref, owner_ref, length_ref, gain_ref,
    collect_ref, place_ref, lane_length_ref, wide_gain_ref, target_ref,
):
    wide_gain_ref[...] = gain_ref[...].astype(F32)
    sessions = session_ref.shape[1]
    slots, places = collect_ref.shape
    me = lax.axis_index("sess")

    def dot(a, b, dims):
        return lax.dot_general(
            a.astype(BF), b.astype(BF), (dims, ((), ())), preferred_element_type=F32
        )

    def one(flag):
        return jnp.where(flag, 1.0, 0.0)

    square = (sessions, sessions)
    before, after = iota(square, 0), iota(square, 1)
    owner_row = jnp.broadcast_to(owner_ref[...], (8, sessions))
    mine = one(owner_row == me)
    slot_of = dot(mine, one(before < after), ((1,), (0,)))
    rows = sessions // blocks
    matches = one(before == session_ref[...])
    row_mine = dot(mine, matches, ((1,), (0,)))
    row_slot = dot(slot_of, matches, ((1,), (0,)))[0:1].astype(I32)
    row_owner = dot(owner_row.astype(F32), matches, ((1,), (0,)))[0:1].astype(I32)
    same_block = (before // rows == after // rows) & (before < after)
    row_pair = dot(row_mine, one(same_block), ((1,), (0,)))[0:1].astype(I32)
    owned = row_mine[0:1] > 0.5
    row_place = row_pair * blocks + iota((1, sessions), 1) // rows
    at_place = (iota((places, sessions), 0) == row_place) & owned
    at_slot = (iota((slots, sessions), 0) == row_slot) & owned
    collect_ref[...] = dot(one(at_slot), one(at_place), ((1,), (1,))).astype(BF)
    place_slot = jnp.sum(jnp.where(at_place, row_slot + 1, 0), axis=1, keepdims=True) - 1
    place_ref[...] = one(place_slot == iota((places, HD), 1) % slots)
    lane_session = one(
        (iota((HD, sessions), 0) % slots == slot_of[0:1].astype(I32)) & (mine[0:1] > 0.5)
    )
    length = jnp.broadcast_to(length_ref[...], (8, sessions))
    high = dot((length >> 4).astype(F32), lane_session, ((1,), (1,)))
    low = dot((length & 15).astype(F32), lane_session, ((1,), (1,)))
    lane_length_ref[...] = (high * 16.0 + low)[0:1].astype(I32)
    local = (rows, sessions)
    row_id = iota(local, 1)
    own_id = me * rows + iota(local, 0)
    own_owner = jnp.sum(jnp.where(row_id == own_id, row_owner, 0), axis=1, keepdims=True)
    earlier = (row_id // rows == me) & (row_id < own_id) & (row_owner == own_owner)
    own_pair = jnp.sum(jnp.where(earlier, 1, 0), axis=1, keepdims=True)
    target_ref[...] = jnp.broadcast_to(own_pair * blocks + own_owner, target_ref.shape)


def turn(tiles):
    row = iota(tiles[0].shape, 0)
    for bit in (4, 2, 1):
        low = (row & bit) == 0
        turned = list(tiles)
        for v in range(8):
            if v & bit == 0:
                a, b = tiles[v], tiles[v + bit]
                turned[v] = jnp.where(low, a, pltpu.roll(b, bit, 0))
                turned[v + bit] = jnp.where(low, pltpu.roll(a, 8 - bit, 0), b)
        tiles = turned
    return tiles


def attend_kernel(
    owners, cap, pieces, x_ref, w_ref, collect_ref, place_ref, length_ref, gain_ref,
    kv_hbm, w_out_hbm, out_ref, kv_ref, w_out_ref, sems, exch_ref, rows_ref, score_ref, sum_ref,
):
    key_copies = []
    for i, first in enumerate(range(0, kv_ref.shape[1], KEY_BLOCK)):
        at = pl.ds(first, min(KEY_BLOCK, kv_ref.shape[1] - first))
        key_copies.append(pltpu.make_async_copy(kv_hbm.at[0, at], kv_ref.at[0, at], sems.at[2 + i]))
    copies = [
        pltpu.make_async_copy(kv_hbm.at[1], kv_ref.at[1], sems.at[0]),
        pltpu.make_async_copy(w_out_hbm, w_out_ref, sems.at[1]),
    ]
    for copy in key_copies + copies:
        copy.start()
    places, model = rows_ref.shape
    span = x_ref.shape[0] // owners
    chunk = cap * pieces
    tiles = model // HD
    context, slots = kv_ref.shape[1], kv_ref.shape[2]
    group = HD // slots
    steps = (context + group) // group
    half = steps // 2

    block = 16 // chunk

    def unpack(i, carry):
        for h in range(owners // 8):
            parts = []
            for o in range(8):
                at = pl.multiple_of((h * 8 + o) * span + i * 16, 16)
                parts.append(x_ref[pl.ds(at, 16), :].astype(F32))
            for b in range(2):
                turned = turn([part[b * 8 : (b + 1) * 8] for part in parts])
                for v, tile in enumerate(turned):
                    row = b * 8 + v
                    t, j, f = row // chunk, row % chunk // pieces, row % pieces
                    k = (i * block + t) * pieces + f
                    exch_ref[k, j * owners + h * 8 : j * owners + h * 8 + 8, :] = tile
        return carry

    lax.fori_loop(0, span // 16, unpack, 0)

    squares = [jnp.zeros((places, HD), F32) for _ in range(2)]
    for k in range(tiles):
        part = exch_ref[k]
        squares[k % 2] += part * part
    scale = lax.rsqrt(jnp.sum(squares[0] + squares[1], axis=1, keepdims=True) / model + 1e-05)
    for k in range(tiles):
        cols = slice(k * HD, (k + 1) * HD)
        rows_ref[:, cols] = (exch_ref[k] * scale * gain_ref[k : k + 1, :]).astype(BF)

    deep = 2 * HD
    sums = [jnp.zeros((places, deep), F32) for _ in range(2)]
    for c in range(model // deep):
        at = slice(c * deep, (c + 1) * deep)
        both = jnp.concatenate([w_ref[0, at, :], w_ref[1, at, :]], axis=1)
        sums[c % 2] += jnp.dot(rows_ref[:, at], both, preferred_element_type=F32)
    for i in range(2):
        sum_ref[i, :places] = sums[i]
    sums = [jnp.zeros((2 * places, deep), F32) for _ in range(2)]
    for c in range(model // deep // 2):
        low = slice(c * deep, (c + 1) * deep)
        high = slice(model // 2 + c * deep, model // 2 + (c + 1) * deep)
        both = jnp.concatenate([w_ref[2, low, :], w_ref[2, high, :]], axis=1)
        stacked = jnp.concatenate([rows_ref[:, low], rows_ref[:, high]], axis=0)
        sums[c % 2] += jnp.dot(stacked, both, preferred_element_type=F32)
    for i in range(2):
        sum_ref[2 + i] = sums[i]
    live = lax.axis_index("sess") >= 0

    @pl.when(live)
    def _():
        query_key = (sum_ref[0, :places] + sum_ref[1, :places]).astype(BF)
        total = sum_ref[2] + sum_ref[3]
        value = (total[:places, :HD] + total[places:, HD:]).astype(BF)
        collect = collect_ref[...]
        query_key = jnp.dot(collect, query_key, preferred_element_type=F32).astype(BF)
        query, new_key = query_key[:, :HD], query_key[:, HD:]
        new_value = jnp.dot(collect, value, preferred_element_type=F32).astype(BF)

        own = iota((slots, HD), 0) == iota((slots, HD), 1) % slots
        for g in range(half):
            first = 2 * g * group
            if first % KEY_BLOCK == 0:
                key_copies[first // KEY_BLOCK].wait()
            last = min(first + 2 * group, context)
            keys = kv_ref[0, first:last].reshape((last - first) * slots, HD)
            if last - first < 2 * group:
                keys = jnp.concatenate([keys, new_key], axis=0)
            dots = lax.dot_general(
                query, keys, (((1,), (1,)), ((), ())), preferred_element_type=F32
            )
            for i in range(2):
                part = jnp.where(own, dots[:, i * HD : (i + 1) * HD], 0.0)
                score_ref[2 * g + i : 2 * g + i + 1, :] = jnp.sum(part, axis=0, keepdims=True)
        scores = score_ref[0:steps, :] * (1.0 / jnp.sqrt(F32(HD)))
        frame = iota((steps, HD), 0) * group + iota((steps, HD), 1) // slots
        valid = (frame < length_ref[...]) | (frame == context)
        scores = jnp.where(valid, scores, -jnp.inf)
        top = jnp.max(scores, axis=0, keepdims=True)
        shift = slots
        while shift < HD:
            top = jnp.maximum(top, pltpu.roll(top, shift, 1))
            shift *= 2
        expo = jnp.where(valid, jnp.exp(scores - top), 0.0)
        total = jnp.sum(expo, axis=0, keepdims=True)
        shift = slots
        while shift < HD:
            total = total + pltpu.roll(total, shift, 1)
            shift *= 2
        score_ref[0:steps, :] = expo / total

        place = place_ref[...] > 0.0

        def weights(step):
            return jnp.where(place, score_ref[step : step + 1, :], 0.0).astype(BF)

        def values(step, count):
            first = step * group
            last = min(first + count * group, context)
            found = kv_ref[1, first:last].reshape((last - first) * slots, HD)
            if last - first < count * group:
                found = jnp.concatenate([found, new_value], axis=0)
            return found

        copies[0].wait()
        sums = [jnp.zeros((2 * places, deep), F32) for _ in range(2)]
        for c in range((half + 1) // 2):
            count = min(2, half - 2 * c)
            left, right = 2 * c, half + 2 * c
            stacked = jnp.concatenate(
                [
                    jnp.concatenate([weights(at + i) for i in range(count)], axis=1)
                    for at in (left, right)
                ],
                axis=0,
            )
            both = jnp.concatenate([values(left, count), values(right, count)], axis=1)
            sums[c % 2] += jnp.dot(stacked, both, preferred_element_type=F32)
        for i in range(2):
            sum_ref[i] = sums[i]

        @pl.when(live)
        def _():
            total = sum_ref[0] + sum_ref[1]
            attended = (total[:places, :HD] + total[places:, HD:]).astype(BF)
            copies[1].wait()
            width = pieces * HD
            for i in range(span // 16):
                found = [
                    jnp.dot(
                        attended,
                        w_out_ref[:, (i * block + t) * width : (i * block + t + 1) * width],
                        preferred_element_type=F32,
                    )
                    for t in range(block)
                ]
                for h in range(owners // 8):
                    turned = []
                    for b in range(2):
                        tiles_in = []
                        for v in range(8):
                            row = b * 8 + v
                            t, j, f = row // chunk, row % chunk // pieces, row % pieces
                            first = j * owners + h * 8
                            tiles_in.append(found[t][first : first + 8, f * HD : (f + 1) * HD])
                        turned.append(turn(tiles_in))
                    for o in range(8):
                        at = (h * 8 + o) * span + i * 16
                        both = jnp.concatenate([turned[0][o], turned[1][o]], axis=0)
                        out_ref[at : at + 16, :] = both.astype(BF)


def attend_scratch(cache, w_out, exchange, tiles, places, model, steps):
    return [
        pltpu.VMEM(cache, BF),
        pltpu.VMEM(w_out, BF),
        pltpu.SemaphoreType.DMA((2 + pl.cdiv(cache[1], KEY_BLOCK),)),
        pltpu.VMEM((tiles, places, HD), F32),
        pltpu.VMEM((places, model), BF),
        pltpu.VMEM((steps + (-steps) % 8, HD), F32),
        pltpu.VMEM((4, 2 * places, 2 * HD), F32),
    ]


def finish_kernel(owners, cap, parts_ref, frames_ref, target_ref, out_ref, sums_ref):
    rows, width = frames_ref.shape
    pieces = width // HD
    chunk = cap * pieces
    span = parts_ref.shape[0] // owners
    for o in range(owners):
        part = parts_ref[o * span : (o + 1) * span, :].astype(F32)
        part = jnp.sum(part.reshape(span // 8, 8, HD), axis=0)
        shift = chunk
        while shift < 8:
            part = part + pltpu.roll(part, shift, 0)
            shift *= 2
        sums_ref[o * chunk : (o + 1) * chunk, :] = part[:chunk]
    target = target_ref[...]
    found = [jnp.zeros((rows, HD), F32) for _ in range(pieces)]
    for o in range(owners):
        for j in range(cap):
            here = target == j * owners + o
            for f in range(pieces):
                at = o * chunk + j * pieces + f
                found[f] = jnp.where(here, sums_ref[at : at + 1, :], found[f])
    for f in range(pieces):
        cols = slice(f * HD, (f + 1) * HD)
        out_ref[:, cols] = (frames_ref[:, cols].astype(F32) + found[f]).astype(BF)


def exchanged(array):
    return lax.all_to_all(array, ("sess", "tp"), split_axis=0, concat_axis=0, tiled=True)


def body(frames, norm_gain, w_qkv, w_out, kv_cache, frame_session, owner_of, context_len):
    owners = lax.axis_size("sess")
    peers = lax.axis_size("tp")
    rows, width = frames.shape
    slots = kv_cache.shape[1]
    cap = (slots + owners - 1) // owners
    places = owners * cap
    pieces = width // HD
    exchange = (owners * peers * cap * pieces, HD)

    outgoing = pl.pallas_call(
        functools.partial(dispatch_kernel, owners, cap),
        out_shape=pltpu.HBM(exchange, BF),
        in_specs=[HBM, HBM, HBM],
        out_specs=HBM,
        scratch_shapes=[
            pltpu.SMEM(frame_session.shape, I32),
            pltpu.SMEM(owner_of.shape, I32),
            pltpu.VMEM(frames.shape, BF),
            pltpu.VMEM((places * pieces, HD), F32),
            pltpu.VMEM(exchange, BF),
            pltpu.SMEM((owners,), I32),
            pltpu.SemaphoreType.DMA((3,)),
            pltpu.SemaphoreType.DMA((4,)),
        ],
        compiler_params=limit(4),
        name="dispatch",
    )(*far(frame_session, owner_of, frames))
    arrived = exchanged(outgoing)

    tables = pl.pallas_call(
        functools.partial(table_kernel, owners),
        out_shape=(
            pltpu.VMEM((slots, places), BF),
            pltpu.VMEM((places, HD), F32),
            pltpu.VMEM((1, HD), I32),
            pltpu.VMEM((norm_gain.size // HD, HD), F32),
            pltpu.VMEM((rows, HD), I32),
        ),
        in_specs=[VM] * 4,
        out_specs=(VM,) * 5,
        compiler_params=limit(4),
        cost_estimate=pl.CostEstimate(flops=10**9, bytes_accessed=10**6, transcendentals=0),
        name="tables",
    )(
        *[a.reshape(1, -1) for a in (frame_session, owner_of, context_len)],
        norm_gain.reshape(-1, HD),
    )
    *tables, target = tables

    cache = kv_cache.transpose(0, 2, 1, 3)
    steps = (cache.shape[1] + HD // slots) // (HD // slots)
    partial_rows = pl.pallas_call(
        functools.partial(attend_kernel, owners, cap, pieces),
        out_shape=pltpu.VMEM(exchange, BF),
        in_specs=[VM] * 6 + [HBM, HBM],
        out_specs=VM,
        scratch_shapes=attend_scratch(
            cache.shape, w_out.shape, exchange, peers * pieces, places, peers * width, steps
        ),
        compiler_params=limit(10),
        name="attend",
    )(*near(arrived, w_qkv, *tables), *far(cache, w_out))
    parts = exchanged(partial_rows)
    return pl.pallas_call(
        functools.partial(finish_kernel, owners, cap),
        out_shape=jax.ShapeDtypeStruct(frames.shape, frames.dtype),
        in_specs=[VM] * 3,
        out_specs=VM,
        scratch_shapes=[pltpu.VMEM((places * pieces, HD), F32)],
        compiler_params=limit(4),
        name="finish",
    )(*near(parts, frames, target))


def solution(mesh):
    in_specs = (
        P("sess", "tp"),
        P(),
        P(None, None, "tp"),
        P("tp", None),
        P(None, "sess", None, "tp"),
        P(),
        P(),
        P(),
    )
    out_specs = P("sess", "tp")
    return jax.shard_map(body, mesh=mesh, in_specs=in_specs, out_specs=out_specs, check_vma=False)
```

```python
import functools

import jax
import jax.numpy as jnp
from jax import lax
from jax.experimental import pallas as pl
from jax.experimental.pallas import tpu as pltpu
from jax.sharding import PartitionSpec as P

HD = 128
KEY_BLOCK = 192
BF = jnp.bfloat16
F32 = jnp.float32
I32 = jnp.int32
VM = pl.BlockSpec(memory_space=pltpu.VMEM)
HBM = pl.BlockSpec(memory_space=pltpu.HBM)


def near(*arrays):
    return [pltpu.with_memory_space_constraint(a, pltpu.VMEM) for a in arrays]


def far(*arrays):
    return [pltpu.with_memory_space_constraint(a, pltpu.HBM) for a in arrays]


def limit(mib):
    return pltpu.CompilerParams(vmem_limit_bytes=mib << 20)


def iota(shape, dim):
    return lax.broadcasted_iota(I32, shape, dim)


def dispatch_kernel(
    owners, cap, session_hbm, owner_hbm, frames_hbm, session_row, owner_row, length_row, gain_hbm,
    out_hbm, collect_ref, place_ref, lane_length_ref, wide_gain_ref, target_ref, frames_ref,
    session_ref, owner_ref, session_near, owner_near, length_near, gain_near,
    held, out_ref, count_ref, in_sems, out_sems,
):
    pairs = (
        (session_hbm, session_ref), (owner_hbm, owner_ref), (frames_hbm, frames_ref),
        (session_row, session_near), (owner_row, owner_near), (length_row, length_near),
        (gain_hbm, gain_near),
    )
    copies = [pltpu.make_async_copy(a, b, in_sems.at[i]) for i, (a, b) in enumerate(pairs)]
    for copy in copies:
        copy.start()
    rows, width = frames_ref.shape
    pieces = width // HD
    chunk = cap * pieces
    held[...] = jnp.zeros_like(held)
    for o in range(owners):
        count_ref[o] = 0
    for copy in copies:
        copy.wait()
    first = lax.axis_index("sess") * rows
    wide = frames_ref[...].astype(F32)
    for r in range(rows):
        o = owner_ref[session_ref[first + r]]
        pair = count_ref[o]
        count_ref[o] = pair + 1
        for f in range(pieces):
            held[pl.ds(o * chunk + pair * pieces + f, 1), :] = wide[r : r + 1, f * HD : (f + 1) * HD]
    span = out_ref.shape[0] // owners
    parts = out_sems.shape[0]
    sent = []
    for o in range(owners):
        piece = held[o * chunk : (o + 1) * chunk, :]
        tile = jnp.concatenate([piece] * (16 // chunk), axis=0).astype(BF)
        for k in range(span // 16):
            out_ref[o * span + k * 16 : o * span + (k + 1) * 16, :] = tile
        if (o + 1) % (owners // parts) == 0:
            at = pl.ds((o + 1 - owners // parts) * span, owners // parts * span)
            copy = pltpu.make_async_copy(out_ref.at[at], out_hbm.at[at], out_sems.at[o // (owners // parts)])
            copy.start()
            sent.append(copy)

    @pl.when(lax.axis_index("sess") >= 0)
    def _():
        write_tables(
            owners, session_near, owner_near, length_near, gain_near,
            collect_ref, place_ref, lane_length_ref, wide_gain_ref, target_ref,
        )
        for copy in sent:
            copy.wait()


def write_tables(
    blocks, session_ref, owner_ref, length_ref, gain_ref,
    collect_ref, place_ref, lane_length_ref, wide_gain_ref, target_ref,
):
    wide_gain_ref[...] = gain_ref[...].astype(F32)
    sessions = session_ref.shape[1]
    slots, places = collect_ref.shape
    me = lax.axis_index("sess")

    def dot(a, b, dims):
        return lax.dot_general(
            a.astype(BF), b.astype(BF), (dims, ((), ())), preferred_element_type=F32
        )

    def one(flag):
        return jnp.where(flag, 1.0, 0.0)

    square = (sessions, sessions)
    before, after = iota(square, 0), iota(square, 1)
    owner_row = jnp.broadcast_to(owner_ref[...], (8, sessions))
    mine = one(owner_row == me)
    slot_of = dot(mine, one(before < after), ((1,), (0,)))
    rows = sessions // blocks
    matches = one(before == session_ref[...])
    row_mine = dot(mine, matches, ((1,), (0,)))
    row_slot = dot(slot_of, matches, ((1,), (0,)))[0:1].astype(I32)
    row_owner = dot(owner_row.astype(F32), matches, ((1,), (0,)))[0:1].astype(I32)
    same_block = (before // rows == after // rows) & (before < after)
    row_pair = dot(row_mine, one(same_block), ((1,), (0,)))[0:1].astype(I32)
    owned = row_mine[0:1] > 0.5
    row_place = row_pair * blocks + iota((1, sessions), 1) // rows
    at_place = (iota((places, sessions), 0) == row_place) & owned
    at_slot = (iota((slots, sessions), 0) == row_slot) & owned
    collect_ref[...] = dot(one(at_slot), one(at_place), ((1,), (1,))).astype(BF)
    place_slot = jnp.sum(jnp.where(at_place, row_slot + 1, 0), axis=1, keepdims=True) - 1
    place_ref[...] = one(place_slot == iota((places, HD), 1) % slots)
    lane_session = one(
        (iota((HD, sessions), 0) % slots == slot_of[0:1].astype(I32)) & (mine[0:1] > 0.5)
    )
    length = jnp.broadcast_to(length_ref[...], (8, sessions))
    high = dot((length >> 4).astype(F32), lane_session, ((1,), (1,)))
    low = dot((length & 15).astype(F32), lane_session, ((1,), (1,)))
    lane_length_ref[...] = (high * 16.0 + low)[0:1].astype(I32)
    local = (rows, sessions)
    row_id = iota(local, 1)
    own_id = me * rows + iota(local, 0)
    own_owner = jnp.sum(jnp.where(row_id == own_id, row_owner, 0), axis=1, keepdims=True)
    earlier = (row_id // rows == me) & (row_id < own_id) & (row_owner == own_owner)
    own_pair = jnp.sum(jnp.where(earlier, 1, 0), axis=1, keepdims=True)
    target_ref[...] = jnp.broadcast_to(own_pair * blocks + own_owner, target_ref.shape)


def turn(tiles):
    row = iota(tiles[0].shape, 0)
    for bit in (4, 2, 1):
        low = (row & bit) == 0
        turned = list(tiles)
        for v in range(8):
            if v & bit == 0:
                a, b = tiles[v], tiles[v + bit]
                turned[v] = jnp.where(low, a, pltpu.roll(b, bit, 0))
                turned[v + bit] = jnp.where(low, pltpu.roll(a, 8 - bit, 0), b)
        tiles = turned
    return tiles


def attend_kernel(
    owners, cap, pieces, x_ref, w_ref, collect_ref, place_ref, length_ref, gain_ref,
    kv_hbm, w_out_hbm, out_ref, kv_ref, w_out_ref, sems, exch_ref, rows_ref, score_ref, sum_ref,
):
    key_copies = []
    for i, first in enumerate(range(0, kv_ref.shape[1], KEY_BLOCK)):
        at = pl.ds(first, min(KEY_BLOCK, kv_ref.shape[1] - first))
        key_copies.append(pltpu.make_async_copy(kv_hbm.at[0, at], kv_ref.at[0, at], sems.at[2 + i]))
    copies = [
        pltpu.make_async_copy(kv_hbm.at[1], kv_ref.at[1], sems.at[0]),
        pltpu.make_async_copy(w_out_hbm, w_out_ref, sems.at[1]),
    ]
    for copy in key_copies + copies:
        copy.start()
    places, model = rows_ref.shape
    span = x_ref.shape[0] // owners
    chunk = cap * pieces
    tiles = model // HD
    context, slots = kv_ref.shape[1], kv_ref.shape[2]
    group = HD // slots
    steps = (context + group) // group
    half = steps // 2

    block = 16 // chunk

    def unpack(i, carry):
        for h in range(owners // 8):
            parts = []
            for o in range(8):
                at = pl.multiple_of((h * 8 + o) * span + i * 16, 16)
                parts.append(x_ref[pl.ds(at, 16), :].astype(F32))
            for b in range(2):
                turned = turn([part[b * 8 : (b + 1) * 8] for part in parts])
                for v, tile in enumerate(turned):
                    row = b * 8 + v
                    t, j, f = row // chunk, row % chunk // pieces, row % pieces
                    k = (i * block + t) * pieces + f
                    exch_ref[k, j * owners + h * 8 : j * owners + h * 8 + 8, :] = tile
        return carry

    lax.fori_loop(0, span // 16, unpack, 0)

    squares = [jnp.zeros((places, HD), F32) for _ in range(2)]
    for k in range(tiles):
        part = exch_ref[k]
        squares[k % 2] += part * part
    scale = lax.rsqrt(jnp.sum(squares[0] + squares[1], axis=1, keepdims=True) / model + 1e-05)
    for k in range(tiles):
        cols = slice(k * HD, (k + 1) * HD)
        rows_ref[:, cols] = (exch_ref[k] * scale * gain_ref[k : k + 1, :]).astype(BF)

    deep = 2 * HD
    sums = [jnp.zeros((places, deep), F32) for _ in range(2)]
    for c in range(model // deep):
        at = slice(c * deep, (c + 1) * deep)
        both = jnp.concatenate([w_ref[0, at, :], w_ref[1, at, :]], axis=1)
        sums[c % 2] += jnp.dot(rows_ref[:, at], both, preferred_element_type=F32)
    for i in range(2):
        sum_ref[i, :places] = sums[i]
    sums = [jnp.zeros((2 * places, deep), F32) for _ in range(2)]
    for c in range(model // deep // 2):
        low = slice(c * deep, (c + 1) * deep)
        high = slice(model // 2 + c * deep, model // 2 + (c + 1) * deep)
        both = jnp.concatenate([w_ref[2, low, :], w_ref[2, high, :]], axis=1)
        stacked = jnp.concatenate([rows_ref[:, low], rows_ref[:, high]], axis=0)
        sums[c % 2] += jnp.dot(stacked, both, preferred_element_type=F32)
    for i in range(2):
        sum_ref[2 + i] = sums[i]
    live = lax.axis_index("sess") >= 0

    @pl.when(live)
    def _():
        query_key = (sum_ref[0, :places] + sum_ref[1, :places]).astype(BF)
        total = sum_ref[2] + sum_ref[3]
        value = (total[:places, :HD] + total[places:, HD:]).astype(BF)
        collect = collect_ref[...]
        query_key = jnp.dot(collect, query_key, preferred_element_type=F32).astype(BF)
        query, new_key = query_key[:, :HD], query_key[:, HD:]
        new_value = jnp.dot(collect, value, preferred_element_type=F32).astype(BF)

        own = iota((slots, HD), 0) == iota((slots, HD), 1) % slots
        for g in range(half):
            first = 2 * g * group
            if first % KEY_BLOCK == 0:
                key_copies[first // KEY_BLOCK].wait()
            last = min(first + 2 * group, context)
            keys = kv_ref[0, first:last].reshape((last - first) * slots, HD)
            if last - first < 2 * group:
                keys = jnp.concatenate([keys, new_key], axis=0)
            dots = lax.dot_general(
                query, keys, (((1,), (1,)), ((), ())), preferred_element_type=F32
            )
            for i in range(2):
                part = jnp.where(own, dots[:, i * HD : (i + 1) * HD], 0.0)
                score_ref[2 * g + i : 2 * g + i + 1, :] = jnp.sum(part, axis=0, keepdims=True)
        scores = score_ref[0:steps, :] * (1.0 / jnp.sqrt(F32(HD)))
        frame = iota((steps, HD), 0) * group + iota((steps, HD), 1) // slots
        valid = (frame < length_ref[...]) | (frame == context)
        scores = jnp.where(valid, scores, -jnp.inf)
        top = jnp.max(scores, axis=0, keepdims=True)
        shift = slots
        while shift < HD:
            top = jnp.maximum(top, pltpu.roll(top, shift, 1))
            shift *= 2
        expo = jnp.where(valid, jnp.exp(scores - top), 0.0)
        total = jnp.sum(expo, axis=0, keepdims=True)
        shift = slots
        while shift < HD:
            total = total + pltpu.roll(total, shift, 1)
            shift *= 2
        score_ref[0:steps, :] = expo / total

        place = place_ref[...] > 0.0

        def weights(step):
            return jnp.where(place, score_ref[step : step + 1, :], 0.0).astype(BF)

        def values(step, count):
            first = step * group
            last = min(first + count * group, context)
            found = kv_ref[1, first:last].reshape((last - first) * slots, HD)
            if last - first < count * group:
                found = jnp.concatenate([found, new_value], axis=0)
            return found

        copies[0].wait()
        sums = [jnp.zeros((2 * places, deep), F32) for _ in range(2)]
        for c in range((half + 1) // 2):
            count = min(2, half - 2 * c)
            left, right = 2 * c, half + 2 * c
            stacked = jnp.concatenate(
                [
                    jnp.concatenate([weights(at + i) for i in range(count)], axis=1)
                    for at in (left, right)
                ],
                axis=0,
            )
            both = jnp.concatenate([values(left, count), values(right, count)], axis=1)
            sums[c % 2] += jnp.dot(stacked, both, preferred_element_type=F32)
        for i in range(2):
            sum_ref[i] = sums[i]

        @pl.when(live)
        def _():
            total = sum_ref[0] + sum_ref[1]
            attended = (total[:places, :HD] + total[places:, HD:]).astype(BF)
            copies[1].wait()
            width = pieces * HD
            for i in range(span // 16):
                found = [
                    jnp.dot(
                        attended,
                        w_out_ref[:, (i * block + t) * width : (i * block + t + 1) * width],
                        preferred_element_type=F32,
                    )
                    for t in range(block)
                ]
                for h in range(owners // 8):
                    turned = []
                    for b in range(2):
                        tiles_in = []
                        for v in range(8):
                            row = b * 8 + v
                            t, j, f = row // chunk, row % chunk // pieces, row % pieces
                            first = j * owners + h * 8
                            tiles_in.append(found[t][first : first + 8, f * HD : (f + 1) * HD])
                        turned.append(turn(tiles_in))
                    for o in range(8):
                        at = (h * 8 + o) * span + i * 16
                        both = jnp.concatenate([turned[0][o], turned[1][o]], axis=0)
                        out_ref[at : at + 16, :] = both.astype(BF)


def attend_scratch(cache, w_out, exchange, tiles, places, model, steps):
    return [
        pltpu.VMEM(cache, BF),
        pltpu.VMEM(w_out, BF),
        pltpu.SemaphoreType.DMA((2 + pl.cdiv(cache[1], KEY_BLOCK),)),
        pltpu.VMEM((tiles, places, HD), F32),
        pltpu.VMEM((places, model), BF),
        pltpu.VMEM((steps + (-steps) % 8, HD), F32),
        pltpu.VMEM((4, 2 * places, 2 * HD), F32),
    ]


def finish_kernel(owners, cap, parts_ref, frames_ref, target_ref, out_ref, sums_ref):
    rows, width = frames_ref.shape
    pieces = width // HD
    chunk = cap * pieces
    span = parts_ref.shape[0] // owners
    for o in range(owners):
        part = parts_ref[o * span : (o + 1) * span, :].astype(F32)
        part = jnp.sum(part.reshape(span // 8, 8, HD), axis=0)
        shift = chunk
        while shift < 8:
            part = part + pltpu.roll(part, shift, 0)
            shift *= 2
        sums_ref[o * chunk : (o + 1) * chunk, :] = part[:chunk]
    target = target_ref[...]
    found = [jnp.zeros((rows, HD), F32) for _ in range(pieces)]
    for o in range(owners):
        for j in range(cap):
            here = target == j * owners + o
            for f in range(pieces):
                at = o * chunk + j * pieces + f
                found[f] = jnp.where(here, sums_ref[at : at + 1, :], found[f])
    for f in range(pieces):
        cols = slice(f * HD, (f + 1) * HD)
        out_ref[:, cols] = (frames_ref[:, cols].astype(F32) + found[f]).astype(BF)


def exchanged(array):
    return lax.all_to_all(array, ("sess", "tp"), split_axis=0, concat_axis=0, tiled=True)


def body(frames, norm_gain, w_qkv, w_out, kv_cache, frame_session, owner_of, context_len):
    owners = lax.axis_size("sess")
    peers = lax.axis_size("tp")
    rows, width = frames.shape
    slots = kv_cache.shape[1]
    cap = (slots + owners - 1) // owners
    places = owners * cap
    pieces = width // HD
    exchange = (owners * peers * cap * pieces, HD)

    lists = [a.reshape(1, -1) for a in (frame_session, owner_of, context_len)]
    lists.append(norm_gain.reshape(-1, HD))
    outgoing, *tables, target, frames_near = pl.pallas_call(
        functools.partial(dispatch_kernel, owners, cap),
        out_shape=(
            pltpu.HBM(exchange, BF),
            pltpu.VMEM((slots, places), BF),
            pltpu.VMEM((places, HD), F32),
            pltpu.VMEM((1, HD), I32),
            pltpu.VMEM((norm_gain.size // HD, HD), F32),
            pltpu.VMEM((rows, HD), I32),
            pltpu.VMEM(frames.shape, frames.dtype),
        ),
        in_specs=[HBM] * 7,
        out_specs=(HBM,) + (VM,) * 6,
        scratch_shapes=[
            pltpu.SMEM(frame_session.shape, I32),
            pltpu.SMEM(owner_of.shape, I32),
            *[pltpu.VMEM(a.shape, a.dtype) for a in lists],
            pltpu.VMEM((places * pieces, HD), F32),
            pltpu.VMEM(exchange, BF),
            pltpu.SMEM((owners,), I32),
            pltpu.SemaphoreType.DMA((7,)),
            pltpu.SemaphoreType.DMA((4,)),
        ],
        compiler_params=limit(4),
        cost_estimate=pl.CostEstimate(flops=10**9, bytes_accessed=10**7, transcendentals=0),
        name="dispatch",
    )(*far(frame_session, owner_of, frames, *lists))
    arrived = exchanged(outgoing)

    cache = kv_cache.transpose(0, 2, 1, 3)
    steps = (cache.shape[1] + HD // slots) // (HD // slots)
    partial_rows = pl.pallas_call(
        functools.partial(attend_kernel, owners, cap, pieces),
        out_shape=pltpu.VMEM(exchange, BF),
        in_specs=[VM] * 6 + [HBM, HBM],
        out_specs=VM,
        scratch_shapes=attend_scratch(
            cache.shape, w_out.shape, exchange, peers * pieces, places, peers * width, steps
        ),
        compiler_params=limit(10),
        name="attend",
    )(*near(arrived, w_qkv, *tables), *far(cache, w_out))
    parts = exchanged(partial_rows)
    return pl.pallas_call(
        functools.partial(finish_kernel, owners, cap),
        out_shape=jax.ShapeDtypeStruct(frames.shape, frames.dtype),
        in_specs=[VM] * 3,
        out_specs=VM,
        scratch_shapes=[pltpu.VMEM((places * pieces, HD), F32)],
        compiler_params=limit(4),
        name="finish",
    )(*near(parts, frames_near, target))


def solution(mesh):
    in_specs = (
        P("sess", "tp"),
        P(),
        P(None, None, "tp"),
        P("tp", None),
        P(None, "sess", None, "tp"),
        P(),
        P(),
        P(),
    )
    out_specs = P("sess", "tp")
    return jax.shard_map(body, mesh=mesh, in_specs=in_specs, out_specs=out_specs, check_vma=False)
```

```python
import functools

import jax
import jax.numpy as jnp
from jax import lax
from jax.experimental import pallas as pl
from jax.experimental.pallas import tpu as pltpu
from jax.sharding import PartitionSpec as P

HD = 128
KEY_BLOCK = 192
BF = jnp.bfloat16
F32 = jnp.float32
I32 = jnp.int32
VM = pl.BlockSpec(memory_space=pltpu.VMEM)
HBM = pl.BlockSpec(memory_space=pltpu.HBM)


def near(*arrays):
    return [pltpu.with_memory_space_constraint(a, pltpu.VMEM) for a in arrays]


def far(*arrays):
    return [pltpu.with_memory_space_constraint(a, pltpu.HBM) for a in arrays]


def limit(mib):
    return pltpu.CompilerParams(vmem_limit_bytes=mib << 20)


def iota(shape, dim):
    return lax.broadcasted_iota(I32, shape, dim)


def dispatch_kernel(
    owners, cap, session_hbm, owner_hbm, frames_hbm, session_row, owner_row, length_row, gain_hbm,
    out_hbm, collect_ref, place_ref, lane_length_ref, wide_gain_ref, target_ref, frames_ref,
    session_ref, owner_ref, session_near, owner_near, length_near, gain_near,
    held, out_ref, count_ref, in_sems, out_sems,
):
    pairs = (
        (session_hbm, session_ref), (owner_hbm, owner_ref), (frames_hbm, frames_ref),
        (session_row, session_near), (owner_row, owner_near), (length_row, length_near),
        (gain_hbm, gain_near),
    )
    copies = [pltpu.make_async_copy(a, b, in_sems.at[i]) for i, (a, b) in enumerate(pairs)]
    for copy in copies:
        copy.start()
    rows, width = frames_ref.shape
    pieces = width // HD
    chunk = cap * pieces
    held[...] = jnp.zeros_like(held)
    for o in range(owners):
        count_ref[o] = 0
    for copy in copies:
        copy.wait()
    first = lax.axis_index("sess") * rows
    wide = frames_ref[...].astype(F32)
    for r in range(rows):
        o = owner_ref[session_ref[first + r]]
        pair = count_ref[o]
        count_ref[o] = pair + 1
        for f in range(pieces):
            held[pl.ds(o * chunk + pair * pieces + f, 1), :] = wide[r : r + 1, f * HD : (f + 1) * HD]
    span = out_ref.shape[0] // owners
    parts = out_sems.shape[0]
    sent = []
    for o in range(owners):
        piece = held[o * chunk : (o + 1) * chunk, :]
        tile = jnp.concatenate([piece] * (16 // chunk), axis=0).astype(BF)
        for k in range(span // 16):
            out_ref[o * span + k * 16 : o * span + (k + 1) * 16, :] = tile
        if (o + 1) % (owners // parts) == 0:
            at = pl.ds((o + 1 - owners // parts) * span, owners // parts * span)
            copy = pltpu.make_async_copy(out_ref.at[at], out_hbm.at[at], out_sems.at[o // (owners // parts)])
            copy.start()
            sent.append(copy)

    @pl.when(lax.axis_index("sess") >= 0)
    def _():
        write_tables(
            owners, session_near, owner_near, length_near, gain_near,
            collect_ref, place_ref, lane_length_ref, wide_gain_ref, target_ref,
        )
        for copy in sent:
            copy.wait()


def write_tables(
    blocks, session_ref, owner_ref, length_ref, gain_ref,
    collect_ref, place_ref, lane_length_ref, wide_gain_ref, target_ref,
):
    wide_gain_ref[...] = gain_ref[...].astype(F32)
    sessions = session_ref.shape[1]
    slots, places = collect_ref.shape
    me = lax.axis_index("sess")

    def dot(a, b, dims):
        return lax.dot_general(
            a.astype(BF), b.astype(BF), (dims, ((), ())), preferred_element_type=F32
        )

    def one(flag):
        return jnp.where(flag, 1.0, 0.0)

    square = (sessions, sessions)
    before, after = iota(square, 0), iota(square, 1)
    owner_row = jnp.broadcast_to(owner_ref[...], (8, sessions))
    mine = one(owner_row == me)
    slot_of = dot(mine, one(before < after), ((1,), (0,)))
    rows = sessions // blocks
    matches = one(before == session_ref[...])
    row_mine = dot(mine, matches, ((1,), (0,)))
    row_slot = dot(slot_of, matches, ((1,), (0,)))[0:1].astype(I32)
    row_owner = dot(owner_row.astype(F32), matches, ((1,), (0,)))[0:1].astype(I32)
    same_block = (before // rows == after // rows) & (before < after)
    row_pair = dot(row_mine, one(same_block), ((1,), (0,)))[0:1].astype(I32)
    owned = row_mine[0:1] > 0.5
    row_place = row_pair * blocks + iota((1, sessions), 1) // rows
    at_place = (iota((places, sessions), 0) == row_place) & owned
    at_slot = (iota((slots, sessions), 0) == row_slot) & owned
    collect_ref[...] = dot(one(at_slot), one(at_place), ((1,), (1,))).astype(BF)
    place_slot = jnp.sum(jnp.where(at_place, row_slot + 1, 0), axis=1, keepdims=True) - 1
    place_ref[...] = one(place_slot == iota((places, HD), 1) % slots)
    lane_session = one(
        (iota((HD, sessions), 0) % slots == slot_of[0:1].astype(I32)) & (mine[0:1] > 0.5)
    )
    length = jnp.broadcast_to(length_ref[...], (8, sessions))
    high = dot((length >> 4).astype(F32), lane_session, ((1,), (1,)))
    low = dot((length & 15).astype(F32), lane_session, ((1,), (1,)))
    lane_length_ref[...] = (high * 16.0 + low)[0:1].astype(I32)
    local = (rows, sessions)
    row_id = iota(local, 1)
    own_id = me * rows + iota(local, 0)
    own_owner = jnp.sum(jnp.where(row_id == own_id, row_owner, 0), axis=1, keepdims=True)
    earlier = (row_id // rows == me) & (row_id < own_id) & (row_owner == own_owner)
    own_pair = jnp.sum(jnp.where(earlier, 1, 0), axis=1, keepdims=True)
    target_ref[...] = jnp.broadcast_to(own_pair * blocks + own_owner, target_ref.shape)


def turn(tiles):
    row = iota(tiles[0].shape, 0)
    for bit in (4, 2, 1):
        low = (row & bit) == 0
        turned = list(tiles)
        for v in range(8):
            if v & bit == 0:
                a, b = tiles[v], tiles[v + bit]
                turned[v] = jnp.where(low, a, pltpu.roll(b, bit, 0))
                turned[v + bit] = jnp.where(low, pltpu.roll(a, 8 - bit, 0), b)
        tiles = turned
    return tiles


def attend_kernel(
    owners, cap, pieces, x_ref, w_ref, collect_ref, place_ref, length_ref, gain_ref,
    kv_hbm, w_out_hbm, out_ref, kv_ref, w_out_ref, sems, exch_ref, rows_ref, score_ref, sum_ref,
):
    key_copies = []
    for i, first in enumerate(range(0, kv_ref.shape[1], KEY_BLOCK)):
        at = pl.ds(first, min(KEY_BLOCK, kv_ref.shape[1] - first))
        key_copies.append(pltpu.make_async_copy(kv_hbm.at[0, at], kv_ref.at[0, at], sems.at[2 + i]))
    copies = [
        pltpu.make_async_copy(kv_hbm.at[1], kv_ref.at[1], sems.at[0]),
        pltpu.make_async_copy(w_out_hbm, w_out_ref, sems.at[1]),
    ]
    for copy in key_copies:
        copy.start()
    places, model = rows_ref.shape
    span = x_ref.shape[0] // owners
    chunk = cap * pieces
    tiles = model // HD
    context, slots = kv_ref.shape[1], kv_ref.shape[2]
    group = HD // slots
    steps = (context + group) // group
    half = steps // 2

    block = 16 // chunk

    halves = owners // 8

    def unpack(i, carry):
        sums = list(carry)
        for h in range(halves):
            parts = []
            for o in range(8):
                at = pl.multiple_of((h * 8 + o) * span + i * 16, 16)
                parts.append(x_ref[pl.ds(at, 16), :].astype(F32))
            for b in range(2):
                turned = turn([part[b * 8 : (b + 1) * 8] for part in parts])
                for v, tile in enumerate(turned):
                    row = b * 8 + v
                    t, j, f = row // chunk, row % chunk // pieces, row % pieces
                    k = (i * block + t) * pieces + f
                    exch_ref[k, j * owners + h * 8 : j * owners + h * 8 + 8, :] = tile
                    sums[j * halves + h] += tile * tile
        return tuple(sums)

    squares = tuple(jnp.zeros((8, HD), F32) for _ in range(cap * halves))
    squares = jnp.concatenate(lax.fori_loop(0, span // 16, unpack, squares), axis=0)
    scale = lax.rsqrt(jnp.sum(squares, axis=1, keepdims=True) / model + 1e-05)
    for k in range(tiles):
        cols = slice(k * HD, (k + 1) * HD)
        rows_ref[:, cols] = (exch_ref[k] * scale * gain_ref[k : k + 1, :]).astype(BF)

    deep = 2 * HD
    sums = [jnp.zeros((places, deep), F32) for _ in range(2)]
    for c in range(model // deep):
        at = slice(c * deep, (c + 1) * deep)
        both = jnp.concatenate([w_ref[0, at, :], w_ref[1, at, :]], axis=1)
        sums[c % 2] += jnp.dot(rows_ref[:, at], both, preferred_element_type=F32)
    for i in range(2):
        sum_ref[i, :places] = sums[i]
    sums = [jnp.zeros((2 * places, deep), F32) for _ in range(2)]
    for c in range(model // deep // 2):
        low = slice(c * deep, (c + 1) * deep)
        high = slice(model // 2 + c * deep, model // 2 + (c + 1) * deep)
        both = jnp.concatenate([w_ref[2, low, :], w_ref[2, high, :]], axis=1)
        stacked = jnp.concatenate([rows_ref[:, low], rows_ref[:, high]], axis=0)
        sums[c % 2] += jnp.dot(stacked, both, preferred_element_type=F32)
    for i in range(2):
        sum_ref[2 + i] = sums[i]
    live = lax.axis_index("sess") >= 0
    for copy in copies:
        copy.start()

    @pl.when(live)
    def _():
        query_key = (sum_ref[0, :places] + sum_ref[1, :places]).astype(BF)
        total = sum_ref[2] + sum_ref[3]
        value = (total[:places, :HD] + total[places:, HD:]).astype(BF)
        collect = collect_ref[...]
        query_key = jnp.dot(collect, query_key, preferred_element_type=F32).astype(BF)
        query, new_key = query_key[:, :HD], query_key[:, HD:]
        new_value = jnp.dot(collect, value, preferred_element_type=F32).astype(BF)

        own = iota((slots, HD), 0) == iota((slots, HD), 1) % slots
        for g in range(half):
            first = 2 * g * group
            if first % KEY_BLOCK == 0:
                key_copies[first // KEY_BLOCK].wait()
            last = min(first + 2 * group, context)
            keys = kv_ref[0, first:last].reshape((last - first) * slots, HD)
            if last - first < 2 * group:
                keys = jnp.concatenate([keys, new_key], axis=0)
            dots = lax.dot_general(
                query, keys, (((1,), (1,)), ((), ())), preferred_element_type=F32
            )
            for i in range(2):
                part = jnp.where(own, dots[:, i * HD : (i + 1) * HD], 0.0)
                score_ref[2 * g + i : 2 * g + i + 1, :] = jnp.sum(part, axis=0, keepdims=True)
        scores = score_ref[0:steps, :] * (1.0 / jnp.sqrt(F32(HD)))
        frame = iota((steps, HD), 0) * group + iota((steps, HD), 1) // slots
        valid = (frame < length_ref[...]) | (frame == context)
        scores = jnp.where(valid, scores, -jnp.inf)
        top = jnp.max(scores, axis=0, keepdims=True)
        shift = slots
        while shift < HD:
            top = jnp.maximum(top, pltpu.roll(top, shift, 1))
            shift *= 2
        expo = jnp.where(valid, jnp.exp(scores - top), 0.0)
        total = jnp.sum(expo, axis=0, keepdims=True)
        shift = slots
        while shift < HD:
            total = total + pltpu.roll(total, shift, 1)
            shift *= 2
        score_ref[0:steps, :] = expo / total

        place = place_ref[...] > 0.0

        def weights(step):
            return jnp.where(place, score_ref[step : step + 1, :], 0.0).astype(BF)

        def values(step, count):
            first = step * group
            last = min(first + count * group, context)
            found = kv_ref[1, first:last].reshape((last - first) * slots, HD)
            if last - first < count * group:
                found = jnp.concatenate([found, new_value], axis=0)
            return found

        copies[0].wait()
        sums = [jnp.zeros((2 * places, deep), F32) for _ in range(2)]
        for c in range((half + 1) // 2):
            count = min(2, half - 2 * c)
            left, right = 2 * c, half + 2 * c
            stacked = jnp.concatenate(
                [
                    jnp.concatenate([weights(at + i) for i in range(count)], axis=1)
                    for at in (left, right)
                ],
                axis=0,
            )
            both = jnp.concatenate([values(left, count), values(right, count)], axis=1)
            sums[c % 2] += jnp.dot(stacked, both, preferred_element_type=F32)
        for i in range(2):
            sum_ref[i] = sums[i]

        @pl.when(live)
        def _():
            total = sum_ref[0] + sum_ref[1]
            attended = (total[:places, :HD] + total[places:, HD:]).astype(BF)
            copies[1].wait()
            width = pieces * HD
            for i in range(span // 16):
                found = [
                    jnp.dot(
                        attended,
                        w_out_ref[:, (i * block + t) * width : (i * block + t + 1) * width],
                        preferred_element_type=F32,
                    )
                    for t in range(block)
                ]
                for h in range(owners // 8):
                    turned = []
                    for b in range(2):
                        tiles_in = []
                        for v in range(8):
                            row = b * 8 + v
                            t, j, f = row // chunk, row % chunk // pieces, row % pieces
                            first = j * owners + h * 8
                            tiles_in.append(found[t][first : first + 8, f * HD : (f + 1) * HD])
                        turned.append(turn(tiles_in))
                    for o in range(8):
                        at = (h * 8 + o) * span + i * 16
                        both = jnp.concatenate([turned[0][o], turned[1][o]], axis=0)
                        out_ref[at : at + 16, :] = both.astype(BF)


def attend_scratch(cache, w_out, exchange, tiles, places, model, steps):
    return [
        pltpu.VMEM(cache, BF),
        pltpu.VMEM(w_out, BF),
        pltpu.SemaphoreType.DMA((2 + pl.cdiv(cache[1], KEY_BLOCK),)),
        pltpu.VMEM((tiles, places, HD), F32),
        pltpu.VMEM((places, model), BF),
        pltpu.VMEM((steps + (-steps) % 8, HD), F32),
        pltpu.VMEM((4, 2 * places, 2 * HD), F32),
    ]


def finish_kernel(owners, cap, parts_ref, frames_ref, target_ref, out_ref, sums_ref):
    rows, width = frames_ref.shape
    pieces = width // HD
    chunk = cap * pieces
    span = parts_ref.shape[0] // owners
    for o in range(owners):
        part = parts_ref[o * span : (o + 1) * span, :].astype(F32)
        part = jnp.sum(part.reshape(span // 8, 8, HD), axis=0)
        shift = chunk
        while shift < 8:
            part = part + pltpu.roll(part, shift, 0)
            shift *= 2
        sums_ref[o * chunk : (o + 1) * chunk, :] = part[:chunk]
    target = target_ref[...]
    found = [jnp.zeros((rows, HD), F32) for _ in range(pieces)]
    for o in range(owners):
        for j in range(cap):
            here = target == j * owners + o
            for f in range(pieces):
                at = o * chunk + j * pieces + f
                found[f] = jnp.where(here, sums_ref[at : at + 1, :], found[f])
    for f in range(pieces):
        cols = slice(f * HD, (f + 1) * HD)
        out_ref[:, cols] = (frames_ref[:, cols].astype(F32) + found[f]).astype(BF)


def exchanged(array):
    return lax.all_to_all(array, ("sess", "tp"), split_axis=0, concat_axis=0, tiled=True)


def body(frames, norm_gain, w_qkv, w_out, kv_cache, frame_session, owner_of, context_len):
    owners = lax.axis_size("sess")
    peers = lax.axis_size("tp")
    rows, width = frames.shape
    slots = kv_cache.shape[1]
    cap = (slots + owners - 1) // owners
    places = owners * cap
    pieces = width // HD
    exchange = (owners * peers * cap * pieces, HD)

    lists = [a.reshape(1, -1) for a in (frame_session, owner_of, context_len)]
    lists.append(norm_gain.reshape(-1, HD))
    outgoing, *tables, target, frames_near = pl.pallas_call(
        functools.partial(dispatch_kernel, owners, cap),
        out_shape=(
            pltpu.HBM(exchange, BF),
            pltpu.VMEM((slots, places), BF),
            pltpu.VMEM((places, HD), F32),
            pltpu.VMEM((1, HD), I32),
            pltpu.VMEM((norm_gain.size // HD, HD), F32),
            pltpu.VMEM((rows, HD), I32),
            pltpu.VMEM(frames.shape, frames.dtype),
        ),
        in_specs=[HBM] * 7,
        out_specs=(HBM,) + (VM,) * 6,
        scratch_shapes=[
            pltpu.SMEM(frame_session.shape, I32),
            pltpu.SMEM(owner_of.shape, I32),
            *[pltpu.VMEM(a.shape, a.dtype) for a in lists],
            pltpu.VMEM((places * pieces, HD), F32),
            pltpu.VMEM(exchange, BF),
            pltpu.SMEM((owners,), I32),
            pltpu.SemaphoreType.DMA((7,)),
            pltpu.SemaphoreType.DMA((4,)),
        ],
        compiler_params=limit(4),
        cost_estimate=pl.CostEstimate(flops=10**9, bytes_accessed=10**7, transcendentals=0),
        name="dispatch",
    )(*far(frame_session, owner_of, frames, *lists))
    arrived = exchanged(outgoing)

    cache = kv_cache.transpose(0, 2, 1, 3)
    steps = (cache.shape[1] + HD // slots) // (HD // slots)
    partial_rows = pl.pallas_call(
        functools.partial(attend_kernel, owners, cap, pieces),
        out_shape=pltpu.VMEM(exchange, BF),
        in_specs=[VM] * 6 + [HBM, HBM],
        out_specs=VM,
        scratch_shapes=attend_scratch(
            cache.shape, w_out.shape, exchange, peers * pieces, places, peers * width, steps
        ),
        compiler_params=limit(10),
        name="attend",
    )(*near(arrived, w_qkv, *tables), *far(cache, w_out))
    parts = exchanged(partial_rows)
    return pl.pallas_call(
        functools.partial(finish_kernel, owners, cap),
        out_shape=jax.ShapeDtypeStruct(frames.shape, frames.dtype),
        in_specs=[VM] * 3,
        out_specs=VM,
        scratch_shapes=[pltpu.VMEM((places * pieces, HD), F32)],
        compiler_params=limit(4),
        name="finish",
    )(*near(parts, frames_near, target))


def solution(mesh):
    in_specs = (
        P("sess", "tp"),
        P(),
        P(None, None, "tp"),
        P("tp", None),
        P(None, "sess", None, "tp"),
        P(),
        P(),
        P(),
    )
    out_specs = P("sess", "tp")
    return jax.shard_map(body, mesh=mesh, in_specs=in_specs, out_specs=out_specs, check_vma=False)
```
